32 devices in a mesh: groups: 2 (over x), row: 8 (over z, y), col: 2 (over core).
Axes of the slice: x: 2, y: 2, z: 4, core: 2. Of those that a mesh axis runs over, the one named last changes fastest.
Arguments:
- queries: bfloat16 [512, 32, 128], P(('groups', 'row', 'col')), parts along dimension 0, may hold values from -4 to 4
- clauses: bfloat16 [512, 32, 128], P(('groups', 'row', 'col')), parts along dimension 0, may hold values from -4 to 4
- pattern: int32 [32, 16], P('groups'), parts along dimension 0, may hold values from 0 to 1, as said below
- positive: int32 [512], P(('groups', 'row', 'col')), parts along dimension 0, may hold values from 0 to 255, as said below
Outputs:
- per_query: float32 [512], P(('groups', 'row', 'col')), parts along dimension 0
- grad_queries: float32 [512, 32, 128], P(('groups', 'row', 'col')), parts along dimension 0
- grad_clauses: float32 [512, 32, 128], P(('groups', 'row', 'col')), parts along dimension 0
The draws below stay inside these ranges and needn't reach their ends.
There are 2 independent parts, one for each index of `groups`. The reference program is written for one: setup_inputs(seed, part) draws one part's arguments, and reference() takes and returns one part's arrays. A program takes and returns all parts, laid end to end along the dimension named above; each array names one. Nothing has to cross between parts.
Inputs may be any that keep to these rules, and one draw needn't show every extreme that they name: Block a holds rows a * 16 to a * 16 + 15; pattern[a, a] = 1 for every block a. positive is a permutation of the rows, and positive[i] lies in the same block of 16 rows as i.
All inputs are finite; a program needn't handle non-finite values.
Results may differ from the reference program's by a relative error of at most 0.0027.
Values may be sent and summed in bfloat16 or wider, within the bound.
A program may use at most 64 MiB of HBM per device.

```python
import jax
import jax.numpy as jnp
from jax import lax

E = 128
LQ = 32
LC = 32
QDEV = 16
NQ = 256


def draw_pair(key):
    draw_key = jax.random.fold_in(key, 17)
    query_key, clause_key = jax.random.split(draw_key, 2)
    query_draw = jnp.clip(0.35 * jax.random.normal(query_key, (NQ, LQ, E), jnp.float32), -4.0, 4.0)
    clause_draw = jnp.clip(0.35 * jax.random.normal(clause_key, (NQ, LC, E), jnp.float32), -4.0, 4.0)
    return (query_draw, clause_draw)


def draw_queries(key, part):
    return draw_pair(key)[0].astype(jnp.bfloat16)


def draw_clauses(key, part):
    return draw_pair(key)[1].astype(jnp.bfloat16)


def draw_pattern(key, part):
    block_total = NQ // QDEV
    density_key, ticket_key = jax.random.split(jax.random.fold_in(key, 5))
    density = jax.random.randint(density_key, (block_total, 1), 1, 8)
    ticket = jax.random.randint(ticket_key, (block_total, block_total), 0, 16)
    diagonal = jnp.arange(block_total)[:, None] == jnp.arange(block_total)[None, :]
    return jnp.where((ticket < density) | diagonal, 1, 0).astype(jnp.int32)


def draw_positive(key, part):
    block_total = NQ // QDEV
    block_keys = jax.random.split(jax.random.fold_in(key, 11), block_total)
    shuffles = jax.vmap(lambda block_key: jax.random.permutation(block_key, QDEV))(block_keys)
    offsets = jnp.arange(block_total, dtype=jnp.int32)[:, None] * QDEV
    return (shuffles.astype(jnp.int32) + offsets).reshape(NQ).astype(jnp.int32)


def setup_inputs(seed: int = 0, part: int = 0) -> dict:
    seeds = jax.random.split(jax.random.key(seed), 5)
    part_splits = jax.random.split(jax.random.fold_in(seeds[4], part), 5)
    return {
        "queries": draw_queries(jax.random.fold_in(jax.random.fold_in(seeds[4], part), 71), part),
        "clauses": draw_clauses(jax.random.fold_in(jax.random.fold_in(seeds[4], part), 71), part),
        "pattern": draw_pattern(jax.random.fold_in(jax.random.fold_in(seeds[4], part), 71), part),
        "positive": draw_positive(jax.random.fold_in(jax.random.fold_in(seeds[4], part), 71), part),
    }


SHARPNESS = 3.0
FLOOR_VALUE = -1.0e30


def tile_logits(query_tile, clause_tile):
    query_count, query_len, width_feat = query_tile.shape
    clause_count, clause_len = clause_tile.shape[0], clause_tile.shape[1]
    products = lax.dot_general(query_tile.reshape(query_count * query_len, width_feat),
                               clause_tile.reshape(clause_count * clause_len, width_feat),
                               (((1,), (1,)), ((), ())), preferred_element_type=jnp.float32)
    return (products * SHARPNESS).reshape(query_count, query_len, clause_count, clause_len)


def token_lse_of(logits):
    token_summit = jnp.max(logits, axis=3)
    return token_summit + jnp.log(jnp.sum(jnp.exp(logits - token_summit[..., None]), axis=3))


def tile_score(query_tile, clause_tile):
    return jnp.sum(token_lse_of(tile_logits(query_tile, clause_tile)), axis=1) / SHARPNESS


def tile_grads(query_tile, clause_tile, factor_tile):
    logits = tile_logits(query_tile, clause_tile)
    token_lse = token_lse_of(logits)
    weights = jnp.exp(logits - token_lse[..., None]) * factor_tile[:, None, :, None]
    query_count, query_len, width_feat = query_tile.shape
    clause_count, clause_len = clause_tile.shape[0], clause_tile.shape[1]
    weights = weights.reshape(query_count * query_len, clause_count * clause_len).astype(jnp.bfloat16)
    grad_query = jnp.dot(weights, clause_tile.reshape(clause_count * clause_len, width_feat),
                         preferred_element_type=jnp.float32)
    grad_clause = lax.dot_general(weights, query_tile.reshape(query_count * query_len, width_feat),
                                  (((0,), (0,)), ((), ())), preferred_element_type=jnp.float32)
    return grad_query.reshape(query_tile.shape), grad_clause.reshape(clause_tile.shape)


def masked_lse(masked, scored, along):
    summit = jnp.max(masked, axis=along, keepdims=True)
    amount = jnp.sum(jnp.where(scored, jnp.exp(masked - summit), 0.0), axis=along)
    return jnp.squeeze(summit, along) + jnp.log(amount)


def reference(queries, clauses, pattern, positive):
    total_rows = queries.shape[0]
    block_count = pattern.shape[0]
    block_rows = total_rows // block_count
    query_blocks = queries.reshape(block_count, block_rows, queries.shape[1], queries.shape[2])
    clause_blocks = clauses.reshape(block_count, block_rows, clauses.shape[1], clauses.shape[2])
    empty_tile = jnp.zeros((block_rows, block_rows), jnp.float32)

    def score_line(query_index):
        def visit_column(clause_index, score_line_rows):
            score_tile = lax.cond(pattern[query_index, clause_index] > 0,
                                  lambda: tile_score(query_blocks[query_index], clause_blocks[clause_index]),
                                  lambda: empty_tile)
            start_col = (clause_index * block_rows).astype(jnp.int32)
            return lax.dynamic_update_slice(score_line_rows, score_tile, (jnp.int32(0), start_col))
        return lax.fori_loop(0, block_count, visit_column, jnp.zeros((block_rows, total_rows), jnp.float32))

    scores = lax.map(score_line, jnp.arange(block_count, dtype=jnp.int32)).reshape(total_rows, total_rows)
    scored = jnp.repeat(jnp.repeat(pattern > 0, block_rows, axis=0), block_rows, axis=1)
    masked = jnp.where(scored, scores, FLOOR_VALUE)
    row_lse = masked_lse(masked, scored, 1)
    col_lse = masked_lse(masked, scored, 0)
    clause_index_all = jnp.arange(total_rows, dtype=jnp.int32)
    matches = positive[:, None] == clause_index_all[None, :]
    positive_score = jnp.sum(jnp.where(matches, scores, 0.0), axis=1)
    positive_col = jnp.sum(jnp.where(matches, col_lse[None, :], 0.0), axis=1)
    per_query = 0.5 * (row_lse - positive_score) + 0.5 * (positive_col - positive_score)
    factor = 0.5 * (jnp.exp(masked - row_lse[:, None]) + jnp.exp(masked - col_lse[None, :])) - jnp.where(matches, 1.0, 0.0)

    def grad_line(query_index, running):
        grad_queries, grad_clauses = running
        query_tile = query_blocks[query_index]
        start_row = (query_index * block_rows).astype(jnp.int32)

        def visit_column(clause_index, running_pair):
            line_grad, clause_grads = running_pair
            start_col = (clause_index * block_rows).astype(jnp.int32)
            factor_tile = lax.dynamic_slice(factor, (start_row, start_col), (block_rows, block_rows))
            clause_tile = clause_blocks[clause_index]
            query_part, clause_part = lax.cond(
                pattern[query_index, clause_index] > 0,
                lambda: tile_grads(query_tile, clause_tile, factor_tile),
                lambda: (jnp.zeros(query_tile.shape, jnp.float32), jnp.zeros(clause_tile.shape, jnp.float32)))
            current = lax.dynamic_slice_in_dim(clause_grads, start_col, block_rows, 0)
            clause_grads = lax.dynamic_update_slice_in_dim(clause_grads, current + clause_part, start_col, 0)
            return line_grad + query_part, clause_grads

        line_grad, grad_clauses = lax.fori_loop(0, block_count, visit_column,
                                                (jnp.zeros(query_tile.shape, jnp.float32), grad_clauses))
        grad_queries = lax.dynamic_update_slice_in_dim(grad_queries, line_grad, start_row, 0)
        return grad_queries, grad_clauses

    grad_queries, grad_clauses = lax.fori_loop(
        0, block_count, grad_line,
        (jnp.zeros(queries.shape, jnp.float32), jnp.zeros(clauses.shape, jnp.float32)))
    return (per_query, grad_queries, grad_clauses)
```

```python
import functools
import math

import jax
import jax.numpy as jnp
from jax import lax
from jax.experimental import pallas as pl
from jax.experimental.pallas import tpu as pltpu
from jax.sharding import PartitionSpec as P

SHARPNESS = 3.0
FLOOR_VALUE = -1e30
EXP2_SCALE = SHARPNESS * math.log2(math.e)
LN2 = math.log(2.0)
AXES = ("row", "col")
F32 = jnp.float32
BF16 = jnp.bfloat16


def dot(a, b, dims):
    return lax.dot_general(a, b, (dims, ((), ())), preferred_element_type=F32)


def split3(x):
    hi = x.astype(BF16)
    rest = x - hi.astype(F32)
    mid = rest.astype(BF16)
    return hi, mid, (rest - mid.astype(F32)).astype(BF16)


def exact_dot(parts, other, dims):
    hi, mid, low = (dot(part, other, dims) for part in parts)
    return hi + (mid + low)


def token_indicator(count, length):
    width = count * length
    item = lax.broadcasted_iota(jnp.int32, (count, width), 0)
    token = lax.broadcasted_iota(jnp.int32, (count, width), 1)
    start = item * length
    return jnp.where((token >= start) & (token < start + length), 1.0, 0.0).astype(BF16)


def position():
    return lax.axis_index("row") * lax.axis_size("col") + lax.axis_index("col")


def score_kernel(dims, pattern_ref, queries_ref, clauses_ref, mask_ref, out_ref, lse_ref):
    block, length, chunk = dims
    place = position()
    tokens = block * length
    blocks = clauses_ref.shape[0] // tokens
    lse_ref[...] = jnp.zeros_like(lse_ref)

    @pl.loop(0, blocks)
    def _(b):
        @pl.when(pattern_ref[place, b] > 0)
        def _():
            for c in range(block // chunk):
                start = pl.multiple_of(b * tokens + c * chunk * length, chunk * length)
                logits = dot(clauses_ref[pl.ds(start, chunk * length), :], queries_ref[...], ((1,), (1,)))
                logits = logits.reshape(chunk, length, tokens)
                top = jnp.max(logits, axis=1)
                total = jnp.sum(jnp.exp2((logits - top[:, None, :]) * EXP2_SCALE), axis=1)
                lse_ref[pl.ds(pl.multiple_of(b * block + c * chunk, chunk), chunk), :] = (
                    top * SHARPNESS + jnp.log(total)
                )

    indicator = token_indicator(block, length)
    hi, mid, low = split3(lse_ref[...])
    sums = dot(indicator, hi, ((1,), (1,))) + (
        dot(indicator, mid, ((1,), (1,))) + dot(indicator, low, ((1,), (1,)))
    )
    out_ref[...] = jnp.where(mask_ref[...] > 0, sums / SHARPNESS, FLOOR_VALUE)


def softmax_weights(logits, factor, chunk, length):
    logits = logits.reshape(chunk, length, logits.shape[1])
    top = jnp.max(logits, axis=1, keepdims=True)
    raised = jnp.exp2((logits - top) * EXP2_SCALE)
    total = jnp.sum(raised, axis=1)
    weights = raised * (factor / total)[:, None, :]
    return weights.reshape(chunk * length, logits.shape[2]).astype(BF16)


def grad_kernel(
    dims, pattern_ref, queries_ref, clauses_ref, own_q_ref, own_c_ref, scores_ref, positive_ref,
    per_query_ref, grad_q_ref, grad_c_ref,
    row_factor_ref, col_factor_ref, weights_ref, grad_qt_ref,
):
    block, length, chunk = dims
    place = position()
    tokens = block * length
    blocks = clauses_ref.shape[0] // tokens
    own = pl.multiple_of(place * block, block)
    indicator = token_indicator(block, length)
    total_rows = scores_ref.shape[0]

    scores = scores_ref[...]
    row_top = jnp.max(scores, axis=1, keepdims=True)
    row_lse = row_top + jnp.log(jnp.sum(jnp.exp(scores - row_top), axis=1, keepdims=True))
    col_top = jnp.max(scores, axis=0, keepdims=True)
    col_lse = col_top + jnp.log(jnp.sum(jnp.exp(scores - col_top), axis=0, keepdims=True))

    mine = scores_ref[pl.ds(own, block), :]
    mine_top = jnp.max(mine, axis=1, keepdims=True)
    mine_lse = mine_top + jnp.log(jnp.sum(jnp.exp(mine - mine_top), axis=1, keepdims=True))
    positive = positive_ref[...]
    matches = positive == lax.broadcasted_iota(jnp.int32, (block, total_rows), 1)
    positive_score = jnp.sum(jnp.where(matches, mine, 0.0), axis=1, keepdims=True)
    positive_col = jnp.sum(jnp.where(matches, col_lse, 0.0), axis=1, keepdims=True)
    per_query_ref[...] = 0.5 * (mine_lse - positive_score) + 0.5 * (positive_col - positive_score)

    row_factor = 0.5 * (jnp.exp(mine - mine_lse) + jnp.exp(mine - col_lse)) - jnp.where(matches, 1.0, 0.0)
    row_factor_ref[...] = exact_dot(split3(row_factor), indicator, ((0,), (0,)))

    factor = 0.5 * (jnp.exp(scores - row_lse) + jnp.exp(scores - col_lse))
    col_factor_ref[...] = pltpu.roll(factor, total_rows - own, 1)[:, :128]
    local = positive - own == lax.broadcasted_iota(jnp.int32, (block, 128), 1)
    col_factor_ref[pl.ds(own, block), :] = col_factor_ref[pl.ds(own, block), :] - jnp.where(local, 1.0, 0.0)

    grad_qt_ref[...] = jnp.zeros_like(grad_qt_ref)
    grad_c_ref[...] = jnp.zeros_like(grad_c_ref)

    @pl.loop(0, blocks)
    def _(b):
        base = pl.multiple_of(b * tokens, tokens)

        @pl.when(pattern_ref[place, b] > 0)
        def _():
            for c in range(block // chunk):
                start = pl.multiple_of(base + c * chunk * length, chunk * length)
                logits = dot(clauses_ref[pl.ds(start, chunk * length), :], own_q_ref[...], ((1,), (1,)))
                factor_tile = row_factor_ref[pl.ds(pl.multiple_of(b * block + c * chunk, chunk), chunk), :]
                weights_ref[pl.ds(c * chunk * length, chunk * length), :] = softmax_weights(
                    logits, factor_tile, chunk, length
                )
            grad_qt_ref[...] += dot(clauses_ref[pl.ds(base, tokens), :], weights_ref[...], ((0,), (0,)))

        @pl.when(pattern_ref[b, place] > 0)
        def _():
            block_factor = col_factor_ref[pl.ds(pl.multiple_of(b * block, block), block), :][:, :block]
            spread = exact_dot(split3(block_factor), indicator, ((0,), (0,)))
            query_tile = queries_ref[pl.ds(base, tokens), :]
            for c in range(block // chunk):
                logits = dot(own_c_ref[pl.ds(c * chunk * length, chunk * length), :], query_tile, ((1,), (1,)))
                weights_ref[pl.ds(c * chunk * length, chunk * length), :] = softmax_weights(
                    logits, spread[c * chunk : (c + 1) * chunk], chunk, length
                )
            grad_c_ref[...] += dot(weights_ref[...], query_tile, ((1,), (0,)))

    grad_q_ref[...] = grad_qt_ref[...].T


def shards(queries, clauses, pattern, positive):
    block, length, width = queries.shape
    blocks = pattern.shape[0]
    tokens = block * length
    total_rows = blocks * block
    dims = (block, length, 8)
    own_q = queries.reshape(tokens, width)
    own_c = clauses.reshape(tokens, width)
    all_c = lax.all_gather(own_c, AXES, axis=0, tiled=True)
    all_q = lax.all_gather(own_q, AXES, axis=0, tiled=True)
    mask = jnp.repeat(lax.dynamic_slice_in_dim(pattern, lax.axis_index(AXES), 1, 0), block, axis=1)
    smem = pl.BlockSpec(memory_space=pltpu.SMEM)
    vmem = pl.BlockSpec(memory_space=pltpu.VMEM)
    params = pltpu.CompilerParams(vmem_limit_bytes=40 * 1024 * 1024)
    scores = pl.pallas_call(
        functools.partial(score_kernel, dims),
        out_shape=jax.ShapeDtypeStruct((block, total_rows), F32),
        in_specs=[smem, vmem, vmem, vmem],
        out_specs=vmem,
        scratch_shapes=[pltpu.VMEM((total_rows, tokens), F32)],
        compiler_params=params,
        cost_estimate=pl.CostEstimate(flops=2 * 10**9, bytes_accessed=4 * 10**6, transcendentals=2 * 10**6),
        name="scores",
    )(pattern, own_q, all_c, mask)
    all_scores = lax.all_gather(scores, AXES, axis=0, tiled=True)
    per_query, grad_q, grad_c = pl.pallas_call(
        functools.partial(grad_kernel, dims),
        out_shape=(
            jax.ShapeDtypeStruct((block, 1), F32),
            jax.ShapeDtypeStruct((tokens, width), F32),
            jax.ShapeDtypeStruct((tokens, width), F32),
        ),
        in_specs=[smem] + [vmem] * 6,
        out_specs=(vmem, vmem, vmem),
        scratch_shapes=[
            pltpu.VMEM((total_rows, tokens), F32),
            pltpu.VMEM((total_rows, 128), F32),
            pltpu.VMEM((tokens, tokens), BF16),
            pltpu.VMEM((width, tokens), F32),
        ],
        compiler_params=params,
        name="grads",
    )(pattern, all_q, all_c, own_q, own_c, all_scores, positive[:, None])
    return (
        per_query.reshape(block),
        grad_q.reshape(queries.shape),
        grad_c.reshape(clauses.shape),
    )


def solution(mesh):
    rows = P(("groups", "row", "col"), None, None)
    ids = P(("groups", "row", "col"))
    return jax.shard_map(
        shards,
        mesh=mesh,
        in_specs=(rows, rows, P("groups", None), ids),
        out_specs=(ids, rows, rows),
        check_vma=False,
    )
```

```python
import functools
import math

import jax
import jax.numpy as jnp
from jax import lax
from jax.experimental import pallas as pl
from jax.experimental.pallas import tpu as pltpu
from jax.sharding import PartitionSpec as P

SHARPNESS = 3.0
FLOOR_VALUE = -1e30
EXP2_SCALE = SHARPNESS * math.log2(math.e)
LN2 = math.log(2.0)
AXES = ("row", "col")
F32 = jnp.float32
BF16 = jnp.bfloat16


def dot(a, b, dims):
    return lax.dot_general(a, b, (dims, ((), ())), preferred_element_type=F32)


def split3(x):
    hi = x.astype(BF16)
    rest = x - hi.astype(F32)
    mid = rest.astype(BF16)
    return hi, mid, (rest - mid.astype(F32)).astype(BF16)


def exact_dot(parts, other, dims):
    hi, mid, low = (dot(part, other, dims) for part in parts)
    return hi + (mid + low)


def token_indicator(count, length):
    width = count * length
    item = lax.broadcasted_iota(jnp.int32, (count, width), 0)
    token = lax.broadcasted_iota(jnp.int32, (count, width), 1)
    start = item * length
    return jnp.where((token >= start) & (token < start + length), 1.0, 0.0).astype(BF16)


def position():
    return lax.axis_index("row") * lax.axis_size("col") + lax.axis_index("col")


def ring_place(row, count):
    if count != 8:
        return row
    side = row % 2
    return (row // 2) * (1 - side) + (7 - row // 2) * side


def ring_row(place, count):
    if count != 8:
        return place
    side = place // 4
    return 2 * (place * (1 - side) + (7 - place) * side) + side


def gather_kernel(count, rows, *refs):
    arrays = len(rows)
    own, full = refs[:arrays], refs[arrays : 2 * arrays]
    hop_send, hop_recv, push_send, push_recv = refs[2 * arrays :]
    row, core = lax.axis_index("row"), lax.axis_index("col")
    sibling = {"col": 1 - core}
    place = ring_place(row, count)
    ahead = {"row": ring_row((place + 1) % count, count)}
    behind = {"row": ring_row((place + count - 1) % count, count)}
    last = count // 2

    def block_start(a, source):
        return pl.multiple_of((source * 2 + core) * rows[a], rows[a])

    def piece(a, way, step):
        if step < last:
            return 0, rows[a]
        return way * (rows[a] // 2), rows[a] // 2

    def hop(a, way, step):
        shift = step - 1
        origin = (place + count - shift) % count if way == 0 else (place + shift) % count
        offset, size = piece(a, way, step)
        start = block_start(a, ring_row(origin, count)) + offset
        target = full[a].at[pl.ds(start, size), :]
        return pltpu.make_async_remote_copy(
            src_ref=own[a].at[pl.ds(offset, size), :] if step == 1 else target,
            dst_ref=target,
            send_sem=hop_send.at[a, way, step - 1],
            recv_sem=hop_recv.at[a, way, step - 1],
            device_id=ahead if way == 0 else behind,
            device_id_type=pl.DeviceIdType.MESH,
        )

    def push(a, way, step):
        offset, size = piece(a, way, step)
        origin = (place + count - step) % count if way == 0 else (place + step) % count
        target = full[a].at[pl.ds(block_start(a, ring_row(origin, count)) + offset, size), :]
        return pltpu.make_async_remote_copy(
            src_ref=own[a] if step == 0 else target,
            dst_ref=target,
            send_sem=push_send.at[a, way, step],
            recv_sem=push_recv.at[a, way, step],
            device_id=sibling,
            device_id_type=pl.DeviceIdType.MESH,
        )

    barrier = pltpu.get_barrier_semaphore()
    for peer in (ahead, behind, sibling):
        pl.semaphore_signal(barrier, inc=1, device_id=peer, device_id_type=pl.DeviceIdType.MESH)
    pl.semaphore_wait(barrier, 3)

    for a in range(arrays):
        for way in (0, 1):
            hop(a, way, 1).start()
        push(a, 0, 0).start()
    for a in range(arrays):
        full[a][pl.ds(block_start(a, row), rows[a]), :] = own[a][...]
    for step in range(1, last + 1):
        for a in range(arrays):
            for way in (0, 1):
                hop(a, way, step).wait_recv()
                if step < last:
                    hop(a, way, step + 1).start()
                push(a, way, step).start()
    for a in range(arrays):
        push(a, 0, 0).wait()
        for step in range(1, last + 1):
            for way in (0, 1):
                hop(a, way, step).wait_send()
                push(a, way, step).wait()


def gathered(blocks, collective_id, name, *arrays):
    count = lax.axis_size("row")
    steps = count // 2
    vmem = pl.BlockSpec(memory_space=pltpu.VMEM)
    sems = pltpu.SemaphoreType.DMA
    many = len(arrays)
    return pl.pallas_call(
        functools.partial(gather_kernel, count, tuple(a.shape[0] for a in arrays)),
        out_shape=tuple(jax.ShapeDtypeStruct((blocks * a.shape[0], a.shape[1]), a.dtype) for a in arrays),
        in_specs=[vmem] * many,
        out_specs=(vmem,) * many,
        scratch_shapes=[
            sems((many, 2, steps)),
            sems((many, 2, steps)),
            sems((many, 2, steps + 1)),
            sems((many, 2, steps + 1)),
        ],
        compiler_params=pltpu.CompilerParams(
            collective_id=collective_id, has_side_effects=True, vmem_limit_bytes=40 * 1024 * 1024
        ),
        name=name,
    )(*arrays)


def score_kernel(dims, pattern_ref, queries_ref, clauses_ref, mask_ref, out_ref, lse_ref):
    block, length, chunk = dims
    place = position()
    tokens = block * length
    blocks = clauses_ref.shape[0] // tokens
    lse_ref[...] = jnp.zeros_like(lse_ref)

    @pl.loop(0, blocks)
    def _(b):
        @pl.when(pattern_ref[place, b] > 0)
        def _():
            for c in range(block // chunk):
                start = pl.multiple_of(b * tokens + c * chunk * length, chunk * length)
                logits = dot(clauses_ref[pl.ds(start, chunk * length), :], queries_ref[...], ((1,), (1,)))
                logits = logits.reshape(chunk, length, tokens)
                top = jnp.max(logits, axis=1)
                total = jnp.sum(jnp.exp2((logits - top[:, None, :]) * EXP2_SCALE), axis=1)
                lse_ref[pl.ds(pl.multiple_of(b * block + c * chunk, chunk), chunk), :] = (
                    top * SHARPNESS + jnp.log(total)
                )

    indicator = token_indicator(block, length)
    hi, mid, low = split3(lse_ref[...])
    sums = dot(indicator, hi, ((1,), (1,))) + (
        dot(indicator, mid, ((1,), (1,))) + dot(indicator, low, ((1,), (1,)))
    )
    out_ref[...] = jnp.where(mask_ref[...] > 0, sums / SHARPNESS, FLOOR_VALUE)


def softmax_weights(logits, factor, chunk, length):
    logits = logits.reshape(chunk, length, logits.shape[1])
    top = jnp.max(logits, axis=1, keepdims=True)
    raised = jnp.exp2((logits - top) * EXP2_SCALE)
    total = jnp.sum(raised, axis=1)
    weights = raised * (factor / total)[:, None, :]
    return weights.reshape(chunk * length, logits.shape[2]).astype(BF16)


def grad_kernel(
    dims, pattern_ref, queries_ref, clauses_ref, own_q_ref, own_c_ref, scores_ref, positive_ref,
    per_query_ref, grad_q_ref, grad_c_ref,
    row_factor_ref, col_factor_ref, weights_ref, grad_qt_ref,
):
    block, length, chunk = dims
    place = position()
    tokens = block * length
    blocks = clauses_ref.shape[0] // tokens
    own = pl.multiple_of(place * block, block)
    indicator = token_indicator(block, length)
    total_rows = scores_ref.shape[0]

    scores = scores_ref[...]
    row_top = jnp.max(scores, axis=1, keepdims=True)
    row_lse = row_top + jnp.log(jnp.sum(jnp.exp(scores - row_top), axis=1, keepdims=True))
    col_top = jnp.max(scores, axis=0, keepdims=True)
    col_lse = col_top + jnp.log(jnp.sum(jnp.exp(scores - col_top), axis=0, keepdims=True))

    mine = scores_ref[pl.ds(own, block), :]
    mine_top = jnp.max(mine, axis=1, keepdims=True)
    mine_lse = mine_top + jnp.log(jnp.sum(jnp.exp(mine - mine_top), axis=1, keepdims=True))
    positive = positive_ref[...]
    matches = positive == lax.broadcasted_iota(jnp.int32, (block, total_rows), 1)
    positive_score = jnp.sum(jnp.where(matches, mine, 0.0), axis=1, keepdims=True)
    positive_col = jnp.sum(jnp.where(matches, col_lse, 0.0), axis=1, keepdims=True)
    per_query_ref[...] = 0.5 * (mine_lse - positive_score) + 0.5 * (positive_col - positive_score)

    row_factor = 0.5 * (jnp.exp(mine - mine_lse) + jnp.exp(mine - col_lse)) - jnp.where(matches, 1.0, 0.0)
    row_factor_ref[...] = exact_dot(split3(row_factor), indicator, ((0,), (0,)))

    factor = 0.5 * (jnp.exp(scores - row_lse) + jnp.exp(scores - col_lse))
    col_factor_ref[...] = pltpu.roll(factor, total_rows - own, 1)[:, :128]
    local = positive - own == lax.broadcasted_iota(jnp.int32, (block, 128), 1)
    col_factor_ref[pl.ds(own, block), :] = col_factor_ref[pl.ds(own, block), :] - jnp.where(local, 1.0, 0.0)

    grad_qt_ref[...] = jnp.zeros_like(grad_qt_ref)
    grad_c_ref[...] = jnp.zeros_like(grad_c_ref)

    @pl.loop(0, blocks)
    def _(b):
        base = pl.multiple_of(b * tokens, tokens)

        @pl.when(pattern_ref[place, b] > 0)
        def _():
            for c in range(block // chunk):
                start = pl.multiple_of(base + c * chunk * length, chunk * length)
                logits = dot(clauses_ref[pl.ds(start, chunk * length), :], own_q_ref[...], ((1,), (1,)))
                factor_tile = row_factor_ref[pl.ds(pl.multiple_of(b * block + c * chunk, chunk), chunk), :]
                weights_ref[pl.ds(c * chunk * length, chunk * length), :] = softmax_weights(
                    logits, factor_tile, chunk, length
                )
            grad_qt_ref[...] += dot(clauses_ref[pl.ds(base, tokens), :], weights_ref[...], ((0,), (0,)))

        @pl.when(pattern_ref[b, place] > 0)
        def _():
            block_factor = col_factor_ref[pl.ds(pl.multiple_of(b * block, block), block), :][:, :block]
            spread = exact_dot(split3(block_factor), indicator, ((0,), (0,)))
            query_tile = queries_ref[pl.ds(base, tokens), :]
            for c in range(block // chunk):
                logits = dot(own_c_ref[pl.ds(c * chunk * length, chunk * length), :], query_tile, ((1,), (1,)))
                weights_ref[pl.ds(c * chunk * length, chunk * length), :] = softmax_weights(
                    logits, spread[c * chunk : (c + 1) * chunk], chunk, length
                )
            grad_c_ref[...] += dot(weights_ref[...], query_tile, ((1,), (0,)))

    grad_q_ref[...] = grad_qt_ref[...].T


def shards(queries, clauses, pattern, positive):
    block, length, width = queries.shape
    blocks = pattern.shape[0]
    tokens = block * length
    total_rows = blocks * block
    dims = (block, length, 8)
    own_q = queries.reshape(tokens, width)
    own_c = clauses.reshape(tokens, width)
    all_c, all_q = gathered(blocks, 0, "gather_tokens", own_c, own_q)
    mask = jnp.repeat(lax.dynamic_slice_in_dim(pattern, lax.axis_index(AXES), 1, 0), block, axis=1)
    smem = pl.BlockSpec(memory_space=pltpu.SMEM)
    vmem = pl.BlockSpec(memory_space=pltpu.VMEM)
    params = pltpu.CompilerParams(vmem_limit_bytes=40 * 1024 * 1024)
    scores = pl.pallas_call(
        functools.partial(score_kernel, dims),
        out_shape=jax.ShapeDtypeStruct((block, total_rows), F32),
        in_specs=[smem, vmem, vmem, vmem],
        out_specs=vmem,
        scratch_shapes=[pltpu.VMEM((total_rows, tokens), F32)],
        compiler_params=params,
        cost_estimate=pl.CostEstimate(flops=2 * 10**9, bytes_accessed=4 * 10**6, transcendentals=2 * 10**6),
        name="scores",
    )(pattern, own_q, all_c, mask)
    (all_scores,) = gathered(blocks, 1, "gather_scores", scores)
    per_query, grad_q, grad_c = pl.pallas_call(
        functools.partial(grad_kernel, dims),
        out_shape=(
            jax.ShapeDtypeStruct((block, 1), F32),
            jax.ShapeDtypeStruct((tokens, width), F32),
            jax.ShapeDtypeStruct((tokens, width), F32),
        ),
        in_specs=[smem] + [vmem] * 6,
        out_specs=(vmem, vmem, vmem),
        scratch_shapes=[
            pltpu.VMEM((total_rows, tokens), F32),
            pltpu.VMEM((total_rows, 128), F32),
            pltpu.VMEM((tokens, tokens), BF16),
            pltpu.VMEM((width, tokens), F32),
        ],
        compiler_params=params,
        name="grads",
    )(pattern, all_q, all_c, own_q, own_c, all_scores, positive[:, None])
    return (
        per_query.reshape(block),
        grad_q.reshape(queries.shape),
        grad_c.reshape(clauses.shape),
    )


def solution(mesh):
    rows = P(("groups", "row", "col"), None, None)
    ids = P(("groups", "row", "col"))
    return jax.shard_map(
        shards,
        mesh=mesh,
        in_specs=(rows, rows, P("groups", None), ids),
        out_specs=(ids, rows, rows),
        check_vma=False,
    )
```

```python
import functools
import math

import jax
import jax.numpy as jnp
from jax import lax
from jax.experimental import pallas as pl
from jax.experimental.pallas import tpu as pltpu
from jax.sharding import PartitionSpec as P

SHARPNESS = 3.0
FLOOR_VALUE = -1e30
EXP2_SCALE = SHARPNESS * math.log2(math.e)
LN2 = math.log(2.0)
F32 = jnp.float32
BF16 = jnp.bfloat16


def dot(a, b, dims):
    return lax.dot_general(a, b, (dims, ((), ())), preferred_element_type=F32)


def split3(x):
    hi = x.astype(BF16)
    rest = x - hi.astype(F32)
    mid = rest.astype(BF16)
    return hi, mid, (rest - mid.astype(F32)).astype(BF16)


def exact_dot(parts, other, dims):
    hi, mid, low = (dot(part, other, dims) for part in parts)
    return hi + (mid + low)


def token_indicator(count, length):
    width = count * length
    item = lax.broadcasted_iota(jnp.int32, (count, width), 0)
    token = lax.broadcasted_iota(jnp.int32, (count, width), 1)
    start = item * length
    return jnp.where((token >= start) & (token < start + length), 1.0, 0.0).astype(BF16)


def position():
    return lax.axis_index("row") * lax.axis_size("col") + lax.axis_index("col")


def ring_place(row, count):
    if count != 8:
        return row
    side = row % 2
    return (row // 2) * (1 - side) + (7 - row // 2) * side


def ring_row(place, count):
    if count != 8:
        return place
    side = place // 4
    return 2 * (place * (1 - side) + (7 - place) * side) + side


def gather_kernel(
    dims, count, pattern_ref, own_c_ref, own_q_ref, full_c_ref, full_q_ref, full_s_ref,
    mine_ref, lse_ref, hop_send, hop_recv, push_send, push_recv, local_sem,
):
    block, length, chunk = dims
    tokens = block * length
    own = (own_c_ref, own_q_ref, mine_ref)
    full = (full_c_ref, full_q_ref, full_s_ref)
    rows = (tokens, tokens, block)
    clause, query, score = 0, 1, 2
    row, core = lax.axis_index("row"), lax.axis_index("col")
    sibling = {"col": 1 - core}
    place = ring_place(row, count)
    ahead = {"row": ring_row((place + 1) % count, count)}
    behind = {"row": ring_row((place + count - 1) % count, count)}
    last = count // 2

    def source_row(way, step):
        return ring_row((place + count + (2 * way - 1) * step) % count, count)

    def block_start(a, source):
        return pl.multiple_of((source * 2 + core) * rows[a], rows[a])

    def piece(a, way, step):
        if step < last:
            return 0, rows[a]
        return way * (rows[a] // 2), rows[a] // 2

    def hop(a, way, step):
        offset, size = piece(a, way, step)
        start = block_start(a, source_row(way, step - 1)) + offset
        target = full[a].at[pl.ds(start, size), :]
        return pltpu.make_async_remote_copy(
            src_ref=own[a].at[pl.ds(offset, size), :] if step == 1 else target,
            dst_ref=target,
            send_sem=hop_send.at[a, way, step - 1],
            recv_sem=hop_recv.at[a, way, step - 1],
            device_id=ahead if way == 0 else behind,
            device_id_type=pl.DeviceIdType.MESH,
        )

    def push(a, way, step):
        offset, size = piece(a, way, step)
        target = full[a].at[pl.ds(block_start(a, source_row(way, step)) + offset, size), :]
        return pltpu.make_async_remote_copy(
            src_ref=own[a] if step == 0 else target,
            dst_ref=target,
            send_sem=push_send.at[a, way, step],
            recv_sem=push_recv.at[a, way, step],
            device_id=sibling,
            device_id_type=pl.DeviceIdType.MESH,
        )

    def begin(a):
        for way in (0, 1):
            hop(a, way, 1).start()
        push(a, 0, 0).start()

    def advance(a, step):
        for way in (0, 1):
            hop(a, way, step).wait_recv()
            if step < last:
                hop(a, way, step + 1).start()
            push(a, way, step).start()

    def score_block(source, side):
        b = source * 2 + side
        for c in range(block // chunk):
            start = pl.multiple_of(b * tokens + c * chunk * length, chunk * length)
            logits = dot(
                full_c_ref[pl.ds(start, chunk * length), :],
                full_q_ref[pl.ds(block_start(query, row), tokens), :],
                ((1,), (1,)),
            ).reshape(chunk, length, tokens)
            top = jnp.max(logits, axis=1, keepdims=True)
            total = jnp.sum(jnp.exp2((logits - top) * EXP2_SCALE), axis=1)
            lse_ref[pl.ds(pl.multiple_of(b * block + c * chunk, chunk), chunk), :] = (
                top.reshape(chunk, tokens) * SHARPNESS + jnp.log(total)
            )

    def score_arrived(step, side):
        @pl.loop(0, 1 if step == last or step == 0 else 2)
        def _(way):
            score_block(source_row(way, step), side)

    barrier = pltpu.get_barrier_semaphore()
    for peer in (ahead, behind, sibling):
        pl.semaphore_signal(barrier, inc=1, device_id=peer, device_id_type=pl.DeviceIdType.MESH)
    locals_ = [
        pltpu.make_async_copy(own[a], full[a].at[pl.ds(block_start(a, row), tokens), :], local_sem.at[a])
        for a in (clause, query)
    ]
    for copy in locals_:
        copy.start()
    pl.semaphore_wait(barrier, 3)

    begin(clause)
    if last == 1:
        begin(query)
    for copy in locals_:
        copy.wait()
    score_arrived(0, core)
    for step in range(1, last + 1):
        advance(clause, step)
        if step == last - 1:
            begin(query)
        if step == 1:
            push(clause, 0, 0).wait()
        else:
            for way in (0, 1):
                push(clause, way, step - 1).wait()
        score_arrived(step, core)
        score_arrived(step - 1, 1 - core)
    for way in (0, 1):
        push(clause, way, last).wait()
    score_arrived(last, 1 - core)

    blocks = full_c_ref.shape[0] // tokens
    me = row * 2 + core
    lane = lax.broadcasted_iota(jnp.int32, mine_ref.shape, 1)
    mask = jnp.zeros(mine_ref.shape, jnp.int32)
    for b in range(blocks):
        mask = jnp.where((lane >= b * block) & (lane < (b + 1) * block), pattern_ref[me, b], mask)
    indicator = token_indicator(block, length)
    hi, mid, low = split3(lse_ref[...])
    sums = dot(indicator, hi, ((1,), (1,))) + (
        dot(indicator, mid, ((1,), (1,))) + dot(indicator, low, ((1,), (1,)))
    )
    mine_ref[...] = jnp.where(mask > 0, sums / SHARPNESS, FLOOR_VALUE)
    begin(score)
    full_s_ref[pl.ds(block_start(score, row), block), :] = mine_ref[...]

    for step in range(1, last + 1):
        advance(query, step)
        advance(score, step)
    for a in (clause, query, score):
        if a != clause:
            push(a, 0, 0).wait()
        for step in range(1, last + 1):
            for way in (0, 1):
                hop(a, way, step).wait_send()
                if a != clause:
                    push(a, way, step).wait()


def softmax_weights(logits, factor, chunk, length):
    logits = logits.reshape(chunk, length, logits.shape[1])
    top = jnp.max(logits, axis=1, keepdims=True)
    raised = jnp.exp2((logits - top) * EXP2_SCALE)
    total = jnp.sum(raised, axis=1)
    weights = raised * (factor / total)[:, None, :]
    return weights.reshape(chunk * length, logits.shape[2]).astype(BF16)


def grad_kernel(
    dims, pattern_ref, positive_ref, queries_ref, clauses_ref, scores_ref,
    per_query_ref, grad_q_ref, grad_c_ref,
    row_factor_ref, col_factor_ref, weights_ref, grad_qt_ref,
):
    block, length, chunk = dims
    place = position()
    tokens = block * length
    blocks = clauses_ref.shape[0] // tokens
    own = pl.multiple_of(place * block, block)
    own_start = pl.multiple_of(place * tokens, tokens)
    indicator = token_indicator(block, length)
    total_rows = scores_ref.shape[0]

    scores = scores_ref[...]
    row_top = jnp.max(scores, axis=1, keepdims=True)
    row_lse = row_top + jnp.log(jnp.sum(jnp.exp(scores - row_top), axis=1, keepdims=True))
    col_top = jnp.max(scores, axis=0, keepdims=True)
    col_lse = col_top + jnp.log(jnp.sum(jnp.exp(scores - col_top), axis=0, keepdims=True))

    mine = scores_ref[pl.ds(own, block), :]
    mine_top = jnp.max(mine, axis=1, keepdims=True)
    mine_lse = mine_top + jnp.log(jnp.sum(jnp.exp(mine - mine_top), axis=1, keepdims=True))
    item = lax.broadcasted_iota(jnp.int32, (block, 1), 0)
    positive = jnp.zeros((block, 1), jnp.int32)
    for i in range(block):
        positive = jnp.where(item == i, positive_ref[i], positive)
    matches = positive == lax.broadcasted_iota(jnp.int32, (block, total_rows), 1)
    positive_score = jnp.sum(jnp.where(matches, mine, 0.0), axis=1, keepdims=True)
    positive_col = jnp.sum(jnp.where(matches, col_lse, 0.0), axis=1, keepdims=True)
    per_query_ref[...] = 0.5 * (mine_lse - positive_score) + 0.5 * (positive_col - positive_score)

    row_factor = 0.5 * (jnp.exp(mine - mine_lse) + jnp.exp(mine - col_lse)) - jnp.where(matches, 1.0, 0.0)
    row_factor_ref[...] = exact_dot(split3(row_factor), indicator, ((0,), (0,)))

    factor = 0.5 * (jnp.exp(scores - row_lse) + jnp.exp(scores - col_lse))
    col_factor_ref[...] = pltpu.roll(factor, total_rows - own, 1)[:, :128]
    local = positive - own == lax.broadcasted_iota(jnp.int32, (block, 128), 1)
    col_factor_ref[pl.ds(own, block), :] = col_factor_ref[pl.ds(own, block), :] - jnp.where(local, 1.0, 0.0)

    grad_qt_ref[...] = jnp.zeros_like(grad_qt_ref)
    grad_c_ref[...] = jnp.zeros_like(grad_c_ref)

    @pl.loop(0, blocks)
    def _(b):
        base = pl.multiple_of(b * tokens, tokens)

        @pl.when(pattern_ref[place, b] > 0)
        def _():
            for c in range(block // chunk):
                start = pl.multiple_of(base + c * chunk * length, chunk * length)
                logits = dot(clauses_ref[pl.ds(start, chunk * length), :], queries_ref[pl.ds(own_start, tokens), :], ((1,), (1,)))
                factor_tile = row_factor_ref[pl.ds(pl.multiple_of(b * block + c * chunk, chunk), chunk), :]
                weights_ref[pl.ds(c * chunk * length, chunk * length), :] = softmax_weights(
                    logits, factor_tile, chunk, length
                )
            grad_qt_ref[...] += dot(clauses_ref[pl.ds(base, tokens), :], weights_ref[...], ((0,), (0,)))

        @pl.when(pattern_ref[b, place] > 0)
        def _():
            block_factor = col_factor_ref[pl.ds(pl.multiple_of(b * block, block), block), :][:, :block]
            spread = exact_dot(split3(block_factor), indicator, ((0,), (0,)))
            query_tile = queries_ref[pl.ds(base, tokens), :]
            for c in range(block // chunk):
                logits = dot(clauses_ref[pl.ds(pl.multiple_of(own_start + c * chunk * length, chunk * length), chunk * length), :], query_tile, ((1,), (1,)))
                weights_ref[pl.ds(c * chunk * length, chunk * length), :] = softmax_weights(
                    logits, spread[c * chunk : (c + 1) * chunk], chunk, length
                )
            grad_c_ref[...] += dot(weights_ref[...], query_tile, ((1,), (0,)))

    grad_q_ref[...] = grad_qt_ref[...].T


def shards(queries, clauses, pattern, positive):
    block, length, width = queries.shape
    blocks = pattern.shape[0]
    tokens = block * length
    total_rows = blocks * block
    dims = (block, length, 8)
    own_q = queries.reshape(tokens, width)
    own_c = clauses.reshape(tokens, width)
    count = lax.axis_size("row")
    smem = pl.BlockSpec(memory_space=pltpu.SMEM)
    vmem = pl.BlockSpec(memory_space=pltpu.VMEM)
    anywhere = pl.BlockSpec(memory_space=pl.ANY)
    sems = pltpu.SemaphoreType.DMA
    all_c, all_q, all_scores = pl.pallas_call(
        functools.partial(gather_kernel, dims, count),
        out_shape=(
            jax.ShapeDtypeStruct((blocks * tokens, width), BF16),
            jax.ShapeDtypeStruct((blocks * tokens, width), BF16),
            jax.ShapeDtypeStruct((total_rows, total_rows), F32),
        ),
        in_specs=[smem, anywhere, anywhere],
        out_specs=(vmem, vmem, vmem),
        scratch_shapes=[
            pltpu.VMEM((block, total_rows), F32),
            pltpu.VMEM((total_rows, tokens), F32),
            sems((3, 2, count // 2)),
            sems((3, 2, count // 2)),
            sems((3, 2, count // 2 + 1)),
            sems((3, 2, count // 2 + 1)),
            sems((2,)),
        ],
        compiler_params=pltpu.CompilerParams(
            collective_id=0, has_side_effects=True, vmem_limit_bytes=40 * 1024 * 1024
        ),
        name="gather_scores",
    )(pattern, own_c, own_q)
    per_query, grad_q, grad_c = pl.pallas_call(
        functools.partial(grad_kernel, dims),
        out_shape=(
            jax.ShapeDtypeStruct((block, 1), F32),
            jax.ShapeDtypeStruct((tokens, width), F32),
            jax.ShapeDtypeStruct((tokens, width), F32),
        ),
        in_specs=[smem, smem, vmem, vmem, vmem],
        out_specs=(vmem, vmem, vmem),
        scratch_shapes=[
            pltpu.VMEM((total_rows, tokens), F32),
            pltpu.VMEM((total_rows, 128), F32),
            pltpu.VMEM((tokens, tokens), BF16),
            pltpu.VMEM((width, tokens), F32),
        ],
        compiler_params=pltpu.CompilerParams(vmem_limit_bytes=40 * 1024 * 1024),
        name="grads",
    )(pattern, positive, all_q, all_c, all_scores)
    return (
        per_query.reshape(block),
        grad_q.reshape(queries.shape),
        grad_c.reshape(clauses.shape),
    )


def solution(mesh):
    rows = P(("groups", "row", "col"), None, None)
    ids = P(("groups", "row", "col"))
    return jax.shard_map(
        shards,
        mesh=mesh,
        in_specs=(rows, rows, P("groups", None), ids),
        out_specs=(ids, rows, rows),
        check_vma=False,
    )
```

```python
import functools
import math

import jax
import jax.numpy as jnp
from jax import lax
from jax.experimental import pallas as pl
from jax.experimental.pallas import tpu as pltpu
from jax.sharding import PartitionSpec as P

SHARPNESS = 3.0
FLOOR_VALUE = -1e30
EXP2_SCALE = SHARPNESS * math.log2(math.e)
LN2 = math.log(2.0)
F32 = jnp.float32
BF16 = jnp.bfloat16


def dot(a, b, dims):
    return lax.dot_general(a, b, (dims, ((), ())), preferred_element_type=F32)


def split3(x):
    hi = x.astype(BF16)
    rest = x - hi.astype(F32)
    mid = rest.astype(BF16)
    return hi, mid, (rest - mid.astype(F32)).astype(BF16)


def exact_dot(parts, other, dims):
    hi, mid, low = (dot(part, other, dims) for part in parts)
    return hi + (mid + low)


def token_indicator(count, length):
    width = count * length
    item = lax.broadcasted_iota(jnp.int32, (count, width), 0)
    token = lax.broadcasted_iota(jnp.int32, (count, width), 1)
    start = item * length
    return jnp.where((token >= start) & (token < start + length), 1.0, 0.0).astype(BF16)


def position():
    return lax.axis_index("row") * lax.axis_size("col") + lax.axis_index("col")


def ring_place(row, count):
    if count != 8:
        return row
    side = row % 2
    return (row // 2) * (1 - side) + (7 - row // 2) * side


def ring_row(place, count):
    if count != 8:
        return place
    side = place // 4
    return 2 * (place * (1 - side) + (7 - place) * side) + side


def gather_kernel(
    dims, count, pattern_ref, own_c_ref, own_q_ref, full_c_ref, full_q_ref, full_s_ref,
    mine_ref, lse_ref, hop_send, hop_recv, push_send, push_recv, local_sem, pattern_smem,
):
    block, length, chunk = dims
    tokens = block * length
    own = (own_c_ref, own_q_ref, mine_ref)
    full = (full_c_ref, full_q_ref, full_s_ref)
    rows = (tokens, tokens, block)
    clause, query, score = 0, 1, 2
    row, core = lax.axis_index("row"), lax.axis_index("col")
    sibling = {"col": 1 - core}
    place = ring_place(row, count)
    ahead = {"row": ring_row((place + 1) % count, count)}
    behind = {"row": ring_row((place + count - 1) % count, count)}
    last = count // 2

    def source_row(way, step):
        return ring_row((place + count + (2 * way - 1) * step) % count, count)

    def block_start(a, source):
        return pl.multiple_of((source * 2 + core) * rows[a], rows[a])

    def piece(a, way, step):
        if step < last:
            return 0, rows[a]
        return way * (rows[a] // 2), rows[a] // 2

    def hop(a, way, step):
        offset, size = piece(a, way, step)
        start = block_start(a, source_row(way, step - 1)) + offset
        target = full[a].at[pl.ds(start, size), :]
        return pltpu.make_async_remote_copy(
            src_ref=own[a].at[pl.ds(offset, size), :] if step == 1 else target,
            dst_ref=target,
            send_sem=hop_send.at[a, way, step - 1],
            recv_sem=hop_recv.at[a, way, step - 1],
            device_id=ahead if way == 0 else behind,
            device_id_type=pl.DeviceIdType.MESH,
        )

    def push(a, way, step):
        offset, size = piece(a, way, step)
        target = full[a].at[pl.ds(block_start(a, source_row(way, step)) + offset, size), :]
        return pltpu.make_async_remote_copy(
            src_ref=own[a] if step == 0 else target,
            dst_ref=target,
            send_sem=push_send.at[a, way, step],
            recv_sem=push_recv.at[a, way, step],
            device_id=sibling,
            device_id_type=pl.DeviceIdType.MESH,
        )

    def begin(a):
        for way in (0, 1):
            hop(a, way, 1).start()
        push(a, 0, 0).start()

    def advance(a, step):
        for way in (0, 1):
            hop(a, way, step).wait_recv()
            if step < last:
                hop(a, way, step + 1).start()
            push(a, way, step).start()

    def score_block(source, side):
        b = source * 2 + side
        for c in range(block // chunk):
            start = pl.multiple_of(b * tokens + c * chunk * length, chunk * length)
            logits = dot(
                full_c_ref[pl.ds(start, chunk * length), :],
                full_q_ref[pl.ds(block_start(query, row), tokens), :],
                ((1,), (1,)),
            ).reshape(chunk, length, tokens)
            top = jnp.max(logits, axis=1, keepdims=True)
            total = jnp.sum(jnp.exp2((logits - top) * EXP2_SCALE), axis=1)
            lse_ref[pl.ds(pl.multiple_of(b * block + c * chunk, chunk), chunk), :] = (
                top.reshape(chunk, tokens) * SHARPNESS + jnp.log(total)
            )

    def score_arrived(step, side):
        @pl.loop(0, 1 if step == last or step == 0 else 2)
        def _(way):
            score_block(source_row(way, step), side)

    barrier = pltpu.get_barrier_semaphore()
    for peer in (ahead, behind, sibling):
        pl.semaphore_signal(barrier, inc=1, device_id=peer, device_id_type=pl.DeviceIdType.MESH)
    locals_ = [
        pltpu.make_async_copy(own[a], full[a].at[pl.ds(block_start(a, row), tokens), :], local_sem.at[a])
        for a in (clause, query)
    ]
    pattern_copy = pltpu.make_async_copy(pattern_ref, pattern_smem, local_sem.at[2])
    pattern_copy.start()
    for copy in locals_:
        copy.start()
    pl.semaphore_wait(barrier, 3)

    lag = min(2, last)
    begin(clause)
    for copy in locals_:
        copy.wait()
    score_arrived(0, core)
    for step in range(1, last + 1):
        advance(clause, step)
        if step == 1:
            push(clause, 0, 0).wait()
        else:
            for way in (0, 1):
                push(clause, way, step - 1).wait()
        if step == lag:
            begin(query)
        score_arrived(step, core)
        if step > lag:
            advance(query, step - lag)
        score_arrived(step - 1, 1 - core)
    for way in (0, 1):
        push(clause, way, last).wait()
    score_arrived(last, 1 - core)

    pattern_copy.wait()
    blocks = full_c_ref.shape[0] // tokens
    me = row * 2 + core
    lane = lax.broadcasted_iota(jnp.int32, mine_ref.shape, 1)
    mask = jnp.zeros(mine_ref.shape, jnp.int32)
    for b in range(blocks):
        mask = jnp.where((lane >= b * block) & (lane < (b + 1) * block), pattern_smem[me, b], mask)
    indicator = token_indicator(block, length)
    hi, mid, low = split3(lse_ref[...])
    sums = dot(indicator, hi, ((1,), (1,))) + (
        dot(indicator, mid, ((1,), (1,))) + dot(indicator, low, ((1,), (1,)))
    )
    mine_ref[...] = jnp.where(mask > 0, sums / SHARPNESS, FLOOR_VALUE)
    begin(score)
    full_s_ref[pl.ds(block_start(score, row), block), :] = mine_ref[...]

    for step in range(1, last + 1):
        advance(score, step)
        if step % 2 == 1 and last - lag + 1 + step // 2 <= last:
            advance(query, last - lag + 1 + step // 2)
    for step in range(last - lag + 1 + (last + 1) // 2, last + 1):
        advance(query, step)
    for a in (clause, query, score):
        if a != clause:
            push(a, 0, 0).wait()
        for step in range(1, last + 1):
            for way in (0, 1):
                hop(a, way, step).wait_send()
                if a != clause:
                    push(a, way, step).wait()


def softmax_weights(logits, factor, chunk, length):
    logits = logits.reshape(chunk, length, logits.shape[1])
    top = jnp.max(logits, axis=1, keepdims=True)
    raised = jnp.exp2((logits - top) * EXP2_SCALE)
    total = jnp.sum(raised, axis=1)
    weights = raised * (factor / total)[:, None, :]
    return weights.reshape(chunk * length, logits.shape[2]).astype(BF16)


def grad_kernel(
    dims, pattern_hbm, positive_hbm, queries_ref, clauses_ref, scores_ref,
    per_query_ref, grad_q_ref, grad_c_ref,
    row_factor_ref, col_factor_ref, weights_ref, grad_qt_ref, pattern_ref, positive_ref, local_sem,
):
    pattern_copy = pltpu.make_async_copy(pattern_hbm, pattern_ref, local_sem.at[0])
    positive_copy = pltpu.make_async_copy(positive_hbm, positive_ref, local_sem.at[1])
    pattern_copy.start()
    positive_copy.start()
    block, length, chunk = dims
    place = position()
    tokens = block * length
    blocks = clauses_ref.shape[0] // tokens
    own = pl.multiple_of(place * block, block)
    own_start = pl.multiple_of(place * tokens, tokens)
    indicator = token_indicator(block, length)
    total_rows = scores_ref.shape[0]

    scores = scores_ref[...]
    row_top = jnp.max(scores, axis=1, keepdims=True)
    row_lse = row_top + jnp.log(jnp.sum(jnp.exp(scores - row_top), axis=1, keepdims=True))
    col_top = jnp.max(scores, axis=0, keepdims=True)
    col_lse = col_top + jnp.log(jnp.sum(jnp.exp(scores - col_top), axis=0, keepdims=True))

    mine = scores_ref[pl.ds(own, block), :]
    mine_top = jnp.max(mine, axis=1, keepdims=True)
    mine_lse = mine_top + jnp.log(jnp.sum(jnp.exp(mine - mine_top), axis=1, keepdims=True))
    pattern_copy.wait()
    positive_copy.wait()
    item = lax.broadcasted_iota(jnp.int32, (block, 1), 0)
    positive = jnp.zeros((block, 1), jnp.int32)
    for i in range(block):
        positive = jnp.where(item == i, positive_ref[i], positive)
    matches = positive == lax.broadcasted_iota(jnp.int32, (block, total_rows), 1)
    positive_score = jnp.sum(jnp.where(matches, mine, 0.0), axis=1, keepdims=True)
    positive_col = jnp.sum(jnp.where(matches, col_lse, 0.0), axis=1, keepdims=True)
    per_query = 0.5 * (mine_lse - positive_score) + 0.5 * (positive_col - positive_score)
    per_query_ref[...] = jnp.sum(
        jnp.where(item == lax.broadcasted_iota(jnp.int32, (block, block), 1), per_query, 0.0),
        axis=0,
        keepdims=True,
    )

    row_factor = 0.5 * (jnp.exp(mine - mine_lse) + jnp.exp(mine - col_lse)) - jnp.where(matches, 1.0, 0.0)
    row_factor_ref[...] = exact_dot(split3(row_factor), indicator, ((0,), (0,)))

    factor = 0.5 * (jnp.exp(scores - row_lse) + jnp.exp(scores - col_lse))
    col_factor_ref[...] = pltpu.roll(factor, total_rows - own, 1)[:, :128]
    local = positive - own == lax.broadcasted_iota(jnp.int32, (block, 128), 1)
    col_factor_ref[pl.ds(own, block), :] = col_factor_ref[pl.ds(own, block), :] - jnp.where(local, 1.0, 0.0)

    grad_qt_ref[...] = jnp.zeros_like(grad_qt_ref)
    grad_c_ref[...] = jnp.zeros_like(grad_c_ref)

    @pl.loop(0, blocks)
    def _(b):
        base = pl.multiple_of(b * tokens, tokens)

        @pl.when(pattern_ref[place, b] > 0)
        def _():
            for c in range(block // chunk):
                start = pl.multiple_of(base + c * chunk * length, chunk * length)
                logits = dot(clauses_ref[pl.ds(start, chunk * length), :], queries_ref[pl.ds(own_start, tokens), :], ((1,), (1,)))
                factor_tile = row_factor_ref[pl.ds(pl.multiple_of(b * block + c * chunk, chunk), chunk), :]
                weights_ref[pl.ds(c * chunk * length, chunk * length), :] = softmax_weights(
                    logits, factor_tile, chunk, length
                )
            grad_qt_ref[...] += dot(clauses_ref[pl.ds(base, tokens), :], weights_ref[...], ((0,), (0,)))

        @pl.when(pattern_ref[b, place] > 0)
        def _():
            block_factor = col_factor_ref[pl.ds(pl.multiple_of(b * block, block), block), :][:, :block]
            spread = exact_dot(split3(block_factor), indicator, ((0,), (0,)))
            query_tile = queries_ref[pl.ds(base, tokens), :]
            for c in range(block // chunk):
                logits = dot(clauses_ref[pl.ds(pl.multiple_of(own_start + c * chunk * length, chunk * length), chunk * length), :], query_tile, ((1,), (1,)))
                weights_ref[pl.ds(c * chunk * length, chunk * length), :] = softmax_weights(
                    logits, spread[c * chunk : (c + 1) * chunk], chunk, length
                )
            grad_c_ref[...] += dot(weights_ref[...], query_tile, ((1,), (0,)))

    grad_q_ref[...] = grad_qt_ref[...].T


def shards(queries, clauses, pattern, positive):
    block, length, width = queries.shape
    blocks = pattern.shape[0]
    tokens = block * length
    total_rows = blocks * block
    dims = (block, length, 8)
    own_q = queries.reshape(tokens, width)
    own_c = clauses.reshape(tokens, width)
    count = lax.axis_size("row")
    vmem = pl.BlockSpec(memory_space=pltpu.VMEM)
    anywhere = pl.BlockSpec(memory_space=pltpu.HBM)
    sems = pltpu.SemaphoreType.DMA
    all_c, all_q, all_scores = pl.pallas_call(
        functools.partial(gather_kernel, dims, count),
        out_shape=(
            jax.ShapeDtypeStruct((blocks * tokens, width), BF16),
            jax.ShapeDtypeStruct((blocks * tokens, width), BF16),
            jax.ShapeDtypeStruct((total_rows, total_rows), F32),
        ),
        in_specs=[anywhere] * 3,
        out_specs=(vmem, vmem, vmem),
        scratch_shapes=[
            pltpu.VMEM((block, total_rows), F32),
            pltpu.VMEM((total_rows, tokens), F32),
            sems((3, 2, count // 2)),
            sems((3, 2, count // 2)),
            sems((3, 2, count // 2 + 1)),
            sems((3, 2, count // 2 + 1)),
            sems((3,)),
            pltpu.SMEM(pattern.shape, jnp.int32),
        ],
        compiler_params=pltpu.CompilerParams(
            collective_id=0, has_side_effects=True, vmem_limit_bytes=40 * 1024 * 1024
        ),
        name="gather_scores",
    )(pattern, own_c, own_q)
    per_query, grad_q, grad_c = pl.pallas_call(
        functools.partial(grad_kernel, dims),
        out_shape=(
            jax.ShapeDtypeStruct((1, block), F32),
            jax.ShapeDtypeStruct((tokens, width), F32),
            jax.ShapeDtypeStruct((tokens, width), F32),
        ),
        in_specs=[anywhere, anywhere, vmem, vmem, vmem],
        out_specs=(vmem, vmem, vmem),
        scratch_shapes=[
            pltpu.VMEM((total_rows, tokens), F32),
            pltpu.VMEM((total_rows, 128), F32),
            pltpu.VMEM((tokens, tokens), BF16),
            pltpu.VMEM((width, tokens), F32),
            pltpu.SMEM(pattern.shape, jnp.int32),
            pltpu.SMEM(positive.shape, jnp.int32),
            sems((2,)),
        ],
        compiler_params=pltpu.CompilerParams(vmem_limit_bytes=40 * 1024 * 1024),
        name="grads",
    )(pattern, positive, all_q, all_c, all_scores)
    return (
        per_query.reshape(block),
        grad_q.reshape(queries.shape),
        grad_c.reshape(clauses.shape),
    )


def solution(mesh):
    rows = P(("groups", "row", "col"), None, None)
    ids = P(("groups", "row", "col"))
    return jax.shard_map(
        shards,
        mesh=mesh,
        in_specs=(rows, rows, P("groups", None), ids),
        out_specs=(ids, rows, rows),
        check_vma=False,
    )
```

```python
import functools
import math

import jax
import jax.numpy as jnp
from jax import lax
from jax.experimental import pallas as pl
from jax.experimental.pallas import tpu as pltpu
from jax.sharding import PartitionSpec as P

SHARPNESS = 3.0
FLOOR_VALUE = -1e30
EXP2_SCALE = SHARPNESS * math.log2(math.e)
LN2 = math.log(2.0)
F32 = jnp.float32
BF16 = jnp.bfloat16


def dot(a, b, dims):
    return lax.dot_general(a, b, (dims, ((), ())), preferred_element_type=F32)


def split3(x):
    hi = x.astype(BF16)
    rest = x - hi.astype(F32)
    mid = rest.astype(BF16)
    return hi, mid, (rest - mid.astype(F32)).astype(BF16)


def exact_dot(parts, other, dims):
    hi, mid, low = (dot(part, other, dims) for part in parts)
    return hi + (mid + low)


def token_indicator(count, length):
    width = count * length
    item = lax.broadcasted_iota(jnp.int32, (count, width), 0)
    token = lax.broadcasted_iota(jnp.int32, (count, width), 1)
    start = item * length
    return jnp.where((token >= start) & (token < start + length), 1.0, 0.0).astype(BF16)


def position():
    return lax.axis_index("row") * lax.axis_size("col") + lax.axis_index("col")


def ring_place(row, count):
    if count != 8:
        return row
    side = row % 2
    return (row // 2) * (1 - side) + (7 - row // 2) * side


def ring_row(place, count):
    if count != 8:
        return place
    side = place // 4
    return 2 * (place * (1 - side) + (7 - place) * side) + side


def gather_kernel(
    dims, count, pattern_ref, own_c_ref, own_q_ref, full_c_ref, full_q_ref, full_s_ref,
    mine_ref, lse_ref, hop_send, hop_recv, push_send, push_recv, score_send, score_recv, local_sem, pattern_smem,
):
    block, length, chunk = dims
    tokens = block * length
    own = (own_c_ref, own_q_ref)
    full = (full_c_ref, full_q_ref)
    rows = (tokens, tokens, block)
    clause, query, score = 0, 1, 2
    row, core = lax.axis_index("row"), lax.axis_index("col")
    sibling = {"col": 1 - core}
    place = ring_place(row, count)
    ahead = {"row": ring_row((place + 1) % count, count)}
    behind = {"row": ring_row((place + count - 1) % count, count)}
    last = count // 2

    def source_row(way, step):
        return ring_row((place + count + (2 * way - 1) * step) % count, count)

    def block_start(a, source):
        return pl.multiple_of((source * 2 + core) * rows[a], rows[a])

    def piece(a, way, step):
        if step < last:
            return 0, rows[a]
        return way * (rows[a] // 2), rows[a] // 2

    def hop(a, way, step):
        offset, size = piece(a, way, step)
        start = block_start(a, source_row(way, step - 1)) + offset
        target = full[a].at[pl.ds(start, size), :]
        return pltpu.make_async_remote_copy(
            src_ref=own[a].at[pl.ds(offset, size), :] if step == 1 else target,
            dst_ref=target,
            send_sem=hop_send.at[a, way, step - 1],
            recv_sem=hop_recv.at[a, way, step - 1],
            device_id=ahead if way == 0 else behind,
            device_id_type=pl.DeviceIdType.MESH,
        )

    def push(a, way, step):
        offset, size = piece(a, way, step)
        target = full[a].at[pl.ds(block_start(a, source_row(way, step)) + offset, size), :]
        return pltpu.make_async_remote_copy(
            src_ref=own[a] if step == 0 else target,
            dst_ref=target,
            send_sem=push_send.at[a, way, step],
            recv_sem=push_recv.at[a, way, step],
            device_id=sibling,
            device_id_type=pl.DeviceIdType.MESH,
        )

    def begin(a):
        for way in (0, 1):
            hop(a, way, 1).start()
        push(a, 0, 0).start()

    def advance(a, step):
        for way in (0, 1):
            hop(a, way, step).wait_recv()
            if step < last:
                hop(a, way, step + 1).start()
            push(a, way, step).start()

    def score_block(source, side):
        b = source * 2 + side
        for c in range(block // chunk):
            start = pl.multiple_of(b * tokens + c * chunk * length, chunk * length)
            logits = dot(
                full_c_ref[pl.ds(start, chunk * length), :],
                full_q_ref[pl.ds(block_start(query, row), tokens), :],
                ((1,), (1,)),
            ).reshape(chunk, length, tokens)
            top = jnp.max(logits, axis=1, keepdims=True)
            total = jnp.sum(jnp.exp2((logits - top) * EXP2_SCALE), axis=1)
            lse_ref[pl.ds(pl.multiple_of(b * block + c * chunk, chunk), chunk), :] = (
                top.reshape(chunk, tokens) * SHARPNESS + jnp.log(total)
            )

    def score_arrived(step, side):
        @pl.loop(0, 1 if step == last or step == 0 else 2)
        def _(way):
            score_block(source_row(way, step), side)

    devices = 2 * count
    me = row * 2 + core

    def peer(distance):
        target = (me + distance) % devices
        return {"row": target // 2, "col": target % 2}

    def send_scores(distance):
        return pltpu.make_async_remote_copy(
            src_ref=mine_ref,
            dst_ref=full_s_ref.at[pl.ds(block_start(score, row), block), :],
            send_sem=score_send.at[distance - 1],
            recv_sem=score_recv.at[distance - 1],
            device_id=peer(distance),
            device_id_type=pl.DeviceIdType.MESH,
        )

    barrier = pltpu.get_barrier_semaphore()
    for distance in range(1, devices):
        pl.semaphore_signal(barrier, inc=1, device_id=peer(distance), device_id_type=pl.DeviceIdType.MESH)
    locals_ = [
        pltpu.make_async_copy(own[a], full[a].at[pl.ds(block_start(a, row), tokens), :], local_sem.at[a])
        for a in (clause, query)
    ]
    pattern_copy = pltpu.make_async_copy(pattern_ref, pattern_smem, local_sem.at[2])
    pattern_copy.start()
    for copy in locals_:
        copy.start()
    pl.semaphore_wait(barrier, devices - 1)

    lag = min(2, last)
    begin(clause)
    for copy in locals_:
        copy.wait()
    score_arrived(0, core)
    for step in range(1, last + 1):
        advance(clause, step)
        if step == lag:
            begin(query)
        if step == 1:
            push(clause, 0, 0).wait()
            score_arrived(0, 1 - core)
        score_arrived(step, core)
        if step > lag:
            advance(query, step - lag)
        for way in (0, 1):
            push(clause, way, step).wait()
        score_arrived(step, 1 - core)

    pattern_copy.wait()
    blocks = full_c_ref.shape[0] // tokens
    lane = lax.broadcasted_iota(jnp.int32, mine_ref.shape, 1)
    mask = jnp.zeros(mine_ref.shape, jnp.int32)
    for b in range(blocks):
        mask = jnp.where((lane >= b * block) & (lane < (b + 1) * block), pattern_smem[me, b], mask)
    indicator = token_indicator(block, length)
    hi, mid, low = split3(lse_ref[...])
    sums = dot(indicator, hi, ((1,), (1,))) + (
        dot(indicator, mid, ((1,), (1,))) + dot(indicator, low, ((1,), (1,)))
    )
    mine_ref[...] = jnp.where(mask > 0, sums / SHARPNESS, FLOOR_VALUE)
    for distance in range(1, devices):
        send_scores(distance).start()
    full_s_ref[pl.ds(block_start(score, row), block), :] = mine_ref[...]

    for step in range(last - lag + 1, last + 1):
        advance(query, step)
    for distance in range(1, devices):
        send_scores(distance).wait()
    push(query, 0, 0).wait()
    for step in range(1, last + 1):
        for way in (0, 1):
            hop(clause, way, step).wait_send()
            hop(query, way, step).wait_send()
            push(query, way, step).wait()


def softmax_weights(logits, factor, chunk, length):
    logits = logits.reshape(chunk, length, logits.shape[1])
    top = jnp.max(logits, axis=1, keepdims=True)
    raised = jnp.exp2((logits - top) * EXP2_SCALE)
    total = jnp.sum(raised, axis=1)
    weights = raised * (factor / total)[:, None, :]
    return weights.reshape(chunk * length, logits.shape[2]).astype(BF16)


def grad_kernel(
    dims, pattern_hbm, positive_hbm, queries_ref, clauses_ref, scores_ref,
    per_query_ref, grad_q_ref, grad_c_ref,
    row_factor_ref, col_factor_ref, weights_ref, grad_qt_ref, pattern_ref, positive_ref, local_sem,
):
    pattern_copy = pltpu.make_async_copy(pattern_hbm, pattern_ref, local_sem.at[0])
    positive_copy = pltpu.make_async_copy(positive_hbm, positive_ref, local_sem.at[1])
    pattern_copy.start()
    positive_copy.start()
    block, length, chunk = dims
    place = position()
    tokens = block * length
    blocks = clauses_ref.shape[0] // tokens
    own = pl.multiple_of(place * block, block)
    own_start = pl.multiple_of(place * tokens, tokens)
    indicator = token_indicator(block, length)
    total_rows = scores_ref.shape[0]

    scores = scores_ref[...]
    row_top = jnp.max(scores, axis=1, keepdims=True)
    row_lse = row_top + jnp.log(jnp.sum(jnp.exp(scores - row_top), axis=1, keepdims=True))
    col_top = jnp.max(scores, axis=0, keepdims=True)
    col_lse = col_top + jnp.log(jnp.sum(jnp.exp(scores - col_top), axis=0, keepdims=True))

    mine = scores_ref[pl.ds(own, block), :]
    mine_top = jnp.max(mine, axis=1, keepdims=True)
    mine_lse = mine_top + jnp.log(jnp.sum(jnp.exp(mine - mine_top), axis=1, keepdims=True))
    pattern_copy.wait()
    positive_copy.wait()
    item = lax.broadcasted_iota(jnp.int32, (block, 1), 0)
    positive = jnp.zeros((block, 1), jnp.int32)
    for i in range(block):
        positive = jnp.where(item == i, positive_ref[i], positive)
    matches = positive == lax.broadcasted_iota(jnp.int32, (block, total_rows), 1)
    positive_score = jnp.sum(jnp.where(matches, mine, 0.0), axis=1, keepdims=True)
    positive_col = jnp.sum(jnp.where(matches, col_lse, 0.0), axis=1, keepdims=True)
    per_query = 0.5 * (mine_lse - positive_score) + 0.5 * (positive_col - positive_score)
    per_query_ref[...] = jnp.sum(
        jnp.where(item == lax.broadcasted_iota(jnp.int32, (block, block), 1), per_query, 0.0),
        axis=0,
        keepdims=True,
    )

    row_factor = 0.5 * (jnp.exp(mine - mine_lse) + jnp.exp(mine - col_lse)) - jnp.where(matches, 1.0, 0.0)
    row_factor_ref[...] = exact_dot(split3(row_factor), indicator, ((0,), (0,)))

    factor = 0.5 * (jnp.exp(scores - row_lse) + jnp.exp(scores - col_lse))
    col_factor_ref[...] = pltpu.roll(factor, total_rows - own, 1)[:, :128]
    local = positive - own == lax.broadcasted_iota(jnp.int32, (block, 128), 1)
    col_factor_ref[pl.ds(own, block), :] = col_factor_ref[pl.ds(own, block), :] - jnp.where(local, 1.0, 0.0)

    grad_qt_ref[...] = jnp.zeros_like(grad_qt_ref)
    grad_c_ref[...] = jnp.zeros_like(grad_c_ref)

    @pl.loop(0, blocks)
    def _(b):
        base = pl.multiple_of(b * tokens, tokens)

        @pl.when(pattern_ref[place, b] > 0)
        def _():
            for c in range(block // chunk):
                start = pl.multiple_of(base + c * chunk * length, chunk * length)
                logits = dot(clauses_ref[pl.ds(start, chunk * length), :], queries_ref[pl.ds(own_start, tokens), :], ((1,), (1,)))
                factor_tile = row_factor_ref[pl.ds(pl.multiple_of(b * block + c * chunk, chunk), chunk), :]
                weights_ref[pl.ds(c * chunk * length, chunk * length), :] = softmax_weights(
                    logits, factor_tile, chunk, length
                )
            grad_qt_ref[...] += dot(clauses_ref[pl.ds(base, tokens), :], weights_ref[...], ((0,), (0,)))

        @pl.when(pattern_ref[b, place] > 0)
        def _():
            block_factor = col_factor_ref[pl.ds(pl.multiple_of(b * block, block), block), :][:, :block]
            spread = exact_dot(split3(block_factor), indicator, ((0,), (0,)))
            query_tile = queries_ref[pl.ds(base, tokens), :]
            for c in range(block // chunk):
                logits = dot(clauses_ref[pl.ds(pl.multiple_of(own_start + c * chunk * length, chunk * length), chunk * length), :], query_tile, ((1,), (1,)))
                weights_ref[pl.ds(c * chunk * length, chunk * length), :] = softmax_weights(
                    logits, spread[c * chunk : (c + 1) * chunk], chunk, length
                )
            grad_c_ref[...] += dot(weights_ref[...], query_tile, ((1,), (0,)))

    grad_q_ref[...] = grad_qt_ref[...].T


def shards(queries, clauses, pattern, positive):
    block, length, width = queries.shape
    blocks = pattern.shape[0]
    tokens = block * length
    total_rows = blocks * block
    dims = (block, length, 8)
    own_q = queries.reshape(tokens, width)
    own_c = clauses.reshape(tokens, width)
    count = lax.axis_size("row")
    vmem = pl.BlockSpec(memory_space=pltpu.VMEM)
    anywhere = pl.BlockSpec(memory_space=pltpu.HBM)
    sems = pltpu.SemaphoreType.DMA
    all_c, all_q, all_scores = pl.pallas_call(
        functools.partial(gather_kernel, dims, count),
        out_shape=(
            jax.ShapeDtypeStruct((blocks * tokens, width), BF16),
            jax.ShapeDtypeStruct((blocks * tokens, width), BF16),
            jax.ShapeDtypeStruct((total_rows, total_rows), F32),
        ),
        in_specs=[anywhere] * 3,
        out_specs=(vmem, vmem, vmem),
        scratch_shapes=[
            pltpu.VMEM((block, total_rows), F32),
            pltpu.VMEM((total_rows, tokens), F32),
            sems((2, 2, count // 2)),
            sems((2, 2, count // 2)),
            sems((2, 2, count // 2 + 1)),
            sems((2, 2, count // 2 + 1)),
            sems((blocks - 1,)),
            sems((blocks - 1,)),
            sems((3,)),
            pltpu.SMEM(pattern.shape, jnp.int32),
        ],
        compiler_params=pltpu.CompilerParams(
            collective_id=0, has_side_effects=True, vmem_limit_bytes=40 * 1024 * 1024
        ),
        name="gather_scores",
    )(pattern, own_c, own_q)
    per_query, grad_q, grad_c = pl.pallas_call(
        functools.partial(grad_kernel, dims),
        out_shape=(
            jax.ShapeDtypeStruct((1, block), F32),
            jax.ShapeDtypeStruct((tokens, width), F32),
            jax.ShapeDtypeStruct((tokens, width), F32),
        ),
        in_specs=[anywhere, anywhere, vmem, vmem, vmem],
        out_specs=(vmem, vmem, vmem),
        scratch_shapes=[
            pltpu.VMEM((total_rows, tokens), F32),
            pltpu.VMEM((total_rows, 128), F32),
            pltpu.VMEM((tokens, tokens), BF16),
            pltpu.VMEM((width, tokens), F32),
            pltpu.SMEM(pattern.shape, jnp.int32),
            pltpu.SMEM(positive.shape, jnp.int32),
            sems((2,)),
        ],
        compiler_params=pltpu.CompilerParams(vmem_limit_bytes=40 * 1024 * 1024),
        name="grads",
    )(pattern, positive, all_q, all_c, all_scores)
    return (
        per_query.reshape(block),
        grad_q.reshape(queries.shape),
        grad_c.reshape(clauses.shape),
    )


def solution(mesh):
    rows = P(("groups", "row", "col"), None, None)
    ids = P(("groups", "row", "col"))
    return jax.shard_map(
        shards,
        mesh=mesh,
        in_specs=(rows, rows, P("groups", None), ids),
        out_specs=(ids, rows, rows),
        check_vma=False,
    )
```

```python
import functools
import math

import jax
import jax.numpy as jnp
from jax import lax
from jax.experimental import pallas as pl
from jax.experimental.pallas import tpu as pltpu
from jax.sharding import PartitionSpec as P

SHARPNESS = 3.0
FLOOR_VALUE = -1e30
EXP2_SCALE = SHARPNESS * math.log2(math.e)
LN2 = math.log(2.0)
F32 = jnp.float32
BF16 = jnp.bfloat16


def dot(a, b, dims):
    return lax.dot_general(a, b, (dims, ((), ())), preferred_element_type=F32)


def split3(x):
    hi = x.astype(BF16)
    rest = x - hi.astype(F32)
    mid = rest.astype(BF16)
    return hi, mid, (rest - mid.astype(F32)).astype(BF16)


def exact_dot(parts, other, dims):
    hi, mid, low = (dot(part, other, dims) for part in parts)
    return hi + (mid + low)


def token_indicator(count, length):
    width = count * length
    item = lax.broadcasted_iota(jnp.int32, (count, width), 0)
    token = lax.broadcasted_iota(jnp.int32, (count, width), 1)
    start = item * length
    return jnp.where((token >= start) & (token < start + length), 1.0, 0.0).astype(BF16)


def position():
    return lax.axis_index("row") * lax.axis_size("col") + lax.axis_index("col")


def ring_place(row, count):
    if count != 8:
        return row
    side = row % 2
    return (row // 2) * (1 - side) + (7 - row // 2) * side


def ring_row(place, count):
    if count != 8:
        return place
    side = place // 4
    return 2 * (place * (1 - side) + (7 - place) * side) + side


def gather_kernel(
    dims, count, pattern_ref, own_c_ref, own_q_ref, full_c_ref, full_q_ref, full_s_ref,
    mine_ref, lse_ref, hop_send, hop_recv, push_send, push_recv, score_send, score_recv, local_sem, pattern_smem,
):
    block, length, chunk = dims
    tokens = block * length
    own = (own_c_ref, own_q_ref)
    full = (full_c_ref, full_q_ref)
    rows = (tokens, tokens, block)
    clause, query, score = 0, 1, 2
    row, core = lax.axis_index("row"), lax.axis_index("col")
    sibling = {"col": 1 - core}
    place = ring_place(row, count)
    ahead = {"row": ring_row((place + 1) % count, count)}
    behind = {"row": ring_row((place + count - 1) % count, count)}
    last = count // 2

    def source_row(way, step):
        return ring_row((place + count + (2 * way - 1) * step) % count, count)

    def block_start(a, source):
        return pl.multiple_of((source * 2 + core) * rows[a], rows[a])

    def piece(a, way, step):
        if step < last:
            return 0, rows[a]
        return way * (rows[a] // 2), rows[a] // 2

    def hop(a, way, step):
        offset, size = piece(a, way, step)
        start = block_start(a, source_row(way, step - 1)) + offset
        target = full[a].at[pl.ds(start, size), :]
        return pltpu.make_async_remote_copy(
            src_ref=own[a].at[pl.ds(offset, size), :] if step == 1 else target,
            dst_ref=target,
            send_sem=hop_send.at[a, way, step - 1],
            recv_sem=hop_recv.at[a, way, step - 1],
            device_id=ahead if way == 0 else behind,
            device_id_type=pl.DeviceIdType.MESH,
        )

    def push(a, way, step):
        offset, size = piece(a, way, step)
        target = full[a].at[pl.ds(block_start(a, source_row(way, step)) + offset, size), :]
        return pltpu.make_async_remote_copy(
            src_ref=own[a] if step == 0 else target,
            dst_ref=target,
            send_sem=push_send.at[a, way, step],
            recv_sem=push_recv.at[a, way, step],
            device_id=sibling,
            device_id_type=pl.DeviceIdType.MESH,
        )

    def begin(a):
        for way in (0, 1):
            hop(a, way, 1).start()
        push(a, 0, 0).start()

    def advance(a, step):
        for way in (0, 1):
            hop(a, way, step).wait_recv()
            if step < last:
                hop(a, way, step + 1).start()
            push(a, way, step).start()

    def score_block(source, side):
        b = source * 2 + side
        for c in range(block // chunk):
            start = pl.multiple_of(b * tokens + c * chunk * length, chunk * length)
            logits = dot(
                full_c_ref[pl.ds(start, chunk * length), :],
                full_q_ref[pl.ds(block_start(query, row), tokens), :],
                ((1,), (1,)),
            ).reshape(chunk, length, tokens)
            top = jnp.max(logits, axis=1, keepdims=True)
            total = jnp.sum(jnp.exp2((logits - top) * EXP2_SCALE), axis=1)
            lse_ref[pl.ds(pl.multiple_of(b * block + c * chunk, chunk), chunk), :] = (
                top.reshape(chunk, tokens) * SHARPNESS + jnp.log(total)
            )

    def score_arrived(step, side):
        @pl.loop(0, 1 if step == last or step == 0 else 2)
        def _(way):
            score_block(source_row(way, step), side)

    devices = 2 * count
    me = row * 2 + core

    def peer(distance):
        target = (me + distance) % devices
        return {"row": target // 2, "col": target % 2}

    def send_scores(distance):
        return pltpu.make_async_remote_copy(
            src_ref=mine_ref,
            dst_ref=full_s_ref.at[pl.ds(block_start(score, row), block), :],
            send_sem=score_send.at[distance - 1],
            recv_sem=score_recv.at[distance - 1],
            device_id=peer(distance),
            device_id_type=pl.DeviceIdType.MESH,
        )

    barrier = pltpu.get_barrier_semaphore()
    for distance in range(1, devices):
        pl.semaphore_signal(barrier, inc=1, device_id=peer(distance), device_id_type=pl.DeviceIdType.MESH)
    locals_ = [
        pltpu.make_async_copy(own[a], full[a].at[pl.ds(block_start(a, row), tokens), :], local_sem.at[a])
        for a in (clause, query)
    ]
    pattern_copy = pltpu.make_async_copy(pattern_ref, pattern_smem, local_sem.at[2])
    pattern_copy.start()
    for copy in locals_:
        copy.start()
    pl.semaphore_wait(barrier, devices - 1)

    begin(clause)
    begin(query)
    for copy in locals_:
        copy.wait()
    score_arrived(0, core)
    push(clause, 0, 0).wait()
    score_arrived(0, 1 - core)
    for step in range(1, last + 1):
        advance(clause, step)
        score_arrived(step, core)
        if step < last:
            advance(query, step)
        for way in (0, 1):
            push(clause, way, step).wait()
        score_arrived(step, 1 - core)

    pattern_copy.wait()
    blocks = full_c_ref.shape[0] // tokens
    lane = lax.broadcasted_iota(jnp.int32, mine_ref.shape, 1)
    mask = jnp.zeros(mine_ref.shape, jnp.int32)
    for b in range(blocks):
        mask = jnp.where((lane >= b * block) & (lane < (b + 1) * block), pattern_smem[me, b], mask)
    indicator = token_indicator(block, length)
    hi, mid, low = split3(lse_ref[...])
    sums = dot(indicator, hi, ((1,), (1,))) + (
        dot(indicator, mid, ((1,), (1,))) + dot(indicator, low, ((1,), (1,)))
    )
    mine_ref[...] = jnp.where(mask > 0, sums / SHARPNESS, FLOOR_VALUE)
    for distance in range(1, devices):
        send_scores(distance).start()
    full_s_ref[pl.ds(block_start(score, row), block), :] = mine_ref[...]

    advance(query, last)
    for distance in range(1, devices):
        send_scores(distance).wait()
    push(query, 0, 0).wait()
    for step in range(1, last + 1):
        for way in (0, 1):
            hop(clause, way, step).wait_send()
            hop(query, way, step).wait_send()
            push(query, way, step).wait()


def softmax_weights(logits, factor, chunk, length):
    logits = logits.reshape(chunk, length, logits.shape[1])
    top = jnp.max(logits, axis=1, keepdims=True)
    raised = jnp.exp2((logits - top) * EXP2_SCALE)
    total = jnp.sum(raised, axis=1)
    weights = raised * (factor / total)[:, None, :]
    return weights.reshape(chunk * length, logits.shape[2]).astype(BF16)


def grad_kernel(
    dims, pattern_hbm, positive_hbm, queries_ref, clauses_ref, scores_ref,
    per_query_ref, grad_q_ref, grad_c_ref,
    row_factor_ref, col_factor_ref, weights_ref, grad_qt_ref, pattern_ref, positive_ref, local_sem,
):
    pattern_copy = pltpu.make_async_copy(pattern_hbm, pattern_ref, local_sem.at[0])
    positive_copy = pltpu.make_async_copy(positive_hbm, positive_ref, local_sem.at[1])
    pattern_copy.start()
    positive_copy.start()
    block, length, chunk = dims
    place = position()
    tokens = block * length
    blocks = clauses_ref.shape[0] // tokens
    own = pl.multiple_of(place * block, block)
    own_start = pl.multiple_of(place * tokens, tokens)
    indicator = token_indicator(block, length)
    total_rows = scores_ref.shape[0]

    scores = scores_ref[...]
    row_top = jnp.max(scores, axis=1, keepdims=True)
    row_lse = row_top + jnp.log(jnp.sum(jnp.exp(scores - row_top), axis=1, keepdims=True))
    col_top = jnp.max(scores, axis=0, keepdims=True)
    col_lse = col_top + jnp.log(jnp.sum(jnp.exp(scores - col_top), axis=0, keepdims=True))

    mine = scores_ref[pl.ds(own, block), :]
    mine_top = jnp.max(mine, axis=1, keepdims=True)
    mine_lse = mine_top + jnp.log(jnp.sum(jnp.exp(mine - mine_top), axis=1, keepdims=True))
    pattern_copy.wait()
    positive_copy.wait()
    item = lax.broadcasted_iota(jnp.int32, (block, 1), 0)
    positive = jnp.zeros((block, 1), jnp.int32)
    for i in range(block):
        positive = jnp.where(item == i, positive_ref[i], positive)
    matches = positive == lax.broadcasted_iota(jnp.int32, (block, total_rows), 1)
    positive_score = jnp.sum(jnp.where(matches, mine, 0.0), axis=1, keepdims=True)
    positive_col = jnp.sum(jnp.where(matches, col_lse, 0.0), axis=1, keepdims=True)
    per_query = 0.5 * (mine_lse - positive_score) + 0.5 * (positive_col - positive_score)
    per_query_ref[...] = jnp.sum(
        jnp.where(item == lax.broadcasted_iota(jnp.int32, (block, block), 1), per_query, 0.0),
        axis=0,
        keepdims=True,
    )

    row_factor = 0.5 * (jnp.exp(mine - mine_lse) + jnp.exp(mine - col_lse)) - jnp.where(matches, 1.0, 0.0)
    row_factor_ref[...] = exact_dot(split3(row_factor), indicator, ((0,), (0,)))

    factor = 0.5 * (jnp.exp(scores - row_lse) + jnp.exp(scores - col_lse))
    col_factor_ref[...] = pltpu.roll(factor, total_rows - own, 1)[:, :128]
    local = positive - own == lax.broadcasted_iota(jnp.int32, (block, 128), 1)
    col_factor_ref[pl.ds(own, block), :] = col_factor_ref[pl.ds(own, block), :] - jnp.where(local, 1.0, 0.0)

    grad_qt_ref[...] = jnp.zeros_like(grad_qt_ref)
    grad_c_ref[...] = jnp.zeros_like(grad_c_ref)

    @pl.loop(0, blocks)
    def _(b):
        base = pl.multiple_of(b * tokens, tokens)

        @pl.when(pattern_ref[place, b] > 0)
        def _():
            for c in range(block // chunk):
                start = pl.multiple_of(base + c * chunk * length, chunk * length)
                logits = dot(clauses_ref[pl.ds(start, chunk * length), :], queries_ref[pl.ds(own_start, tokens), :], ((1,), (1,)))
                factor_tile = row_factor_ref[pl.ds(pl.multiple_of(b * block + c * chunk, chunk), chunk), :]
                weights_ref[pl.ds(c * chunk * length, chunk * length), :] = softmax_weights(
                    logits, factor_tile, chunk, length
                )
            grad_qt_ref[...] += dot(clauses_ref[pl.ds(base, tokens), :], weights_ref[...], ((0,), (0,)))

        @pl.when(pattern_ref[b, place] > 0)
        def _():
            block_factor = col_factor_ref[pl.ds(pl.multiple_of(b * block, block), block), :][:, :block]
            spread = exact_dot(split3(block_factor), indicator, ((0,), (0,)))
            query_tile = queries_ref[pl.ds(base, tokens), :]
            for c in range(block // chunk):
                logits = dot(clauses_ref[pl.ds(pl.multiple_of(own_start + c * chunk * length, chunk * length), chunk * length), :], query_tile, ((1,), (1,)))
                weights_ref[pl.ds(c * chunk * length, chunk * length), :] = softmax_weights(
                    logits, spread[c * chunk : (c + 1) * chunk], chunk, length
                )
            grad_c_ref[...] += dot(weights_ref[...], query_tile, ((1,), (0,)))

    grad_q_ref[...] = grad_qt_ref[...].T


def shards(queries, clauses, pattern, positive):
    block, length, width = queries.shape
    blocks = pattern.shape[0]
    tokens = block * length
    total_rows = blocks * block
    dims = (block, length, 8)
    own_q = queries.reshape(tokens, width)
    own_c = clauses.reshape(tokens, width)
    count = lax.axis_size("row")
    vmem = pl.BlockSpec(memory_space=pltpu.VMEM)
    anywhere = pl.BlockSpec(memory_space=pltpu.HBM)
    sems = pltpu.SemaphoreType.DMA
    all_c, all_q, all_scores = pl.pallas_call(
        functools.partial(gather_kernel, dims, count),
        out_shape=(
            jax.ShapeDtypeStruct((blocks * tokens, width), BF16),
            jax.ShapeDtypeStruct((blocks * tokens, width), BF16),
            jax.ShapeDtypeStruct((total_rows, total_rows), F32),
        ),
        in_specs=[anywhere] * 3,
        out_specs=(vmem, vmem, vmem),
        scratch_shapes=[
            pltpu.VMEM((block, total_rows), F32),
            pltpu.VMEM((total_rows, tokens), F32),
            sems((2, 2, count // 2)),
            sems((2, 2, count // 2)),
            sems((2, 2, count // 2 + 1)),
            sems((2, 2, count // 2 + 1)),
            sems((blocks - 1,)),
            sems((blocks - 1,)),
            sems((3,)),
            pltpu.SMEM(pattern.shape, jnp.int32),
        ],
        compiler_params=pltpu.CompilerParams(
            collective_id=0, has_side_effects=True, vmem_limit_bytes=40 * 1024 * 1024
        ),
        name="gather_scores",
    )(pattern, own_c, own_q)
    per_query, grad_q, grad_c = pl.pallas_call(
        functools.partial(grad_kernel, dims),
        out_shape=(
            jax.ShapeDtypeStruct((1, block), F32),
            jax.ShapeDtypeStruct((tokens, width), F32),
            jax.ShapeDtypeStruct((tokens, width), F32),
        ),
        in_specs=[anywhere, anywhere, vmem, vmem, vmem],
        out_specs=(vmem, vmem, vmem),
        scratch_shapes=[
            pltpu.VMEM((total_rows, tokens), F32),
            pltpu.VMEM((total_rows, 128), F32),
            pltpu.VMEM((tokens, tokens), BF16),
            pltpu.VMEM((width, tokens), F32),
            pltpu.SMEM(pattern.shape, jnp.int32),
            pltpu.SMEM(positive.shape, jnp.int32),
            sems((2,)),
        ],
        compiler_params=pltpu.CompilerParams(vmem_limit_bytes=40 * 1024 * 1024),
        name="grads",
    )(pattern, positive, all_q, all_c, all_scores)
    return (
        per_query.reshape(block),
        grad_q.reshape(queries.shape),
        grad_c.reshape(clauses.shape),
    )


def solution(mesh):
    rows = P(("groups", "row", "col"), None, None)
    ids = P(("groups", "row", "col"))
    return jax.shard_map(
        shards,
        mesh=mesh,
        in_specs=(rows, rows, P("groups", None), ids),
        out_specs=(ids, rows, rows),
        check_vma=False,
    )
```

```python
import functools
import math

import jax
import jax.numpy as jnp
from jax import lax
from jax.experimental import pallas as pl
from jax.experimental.pallas import tpu as pltpu
from jax.sharding import PartitionSpec as P

SHARPNESS = 3.0
FLOOR_VALUE = -1e30
EXP2_SCALE = SHARPNESS * math.log2(math.e)
LN2 = math.log(2.0)
F32 = jnp.float32
BF16 = jnp.bfloat16


def dot(a, b, dims):
    return lax.dot_general(a, b, (dims, ((), ())), preferred_element_type=F32)


def split3(x):
    hi = x.astype(BF16)
    rest = x - hi.astype(F32)
    mid = rest.astype(BF16)
    return hi, mid, (rest - mid.astype(F32)).astype(BF16)


def exact_dot(parts, other, dims):
    hi, mid, low = (dot(part, other, dims) for part in parts)
    return hi + (mid + low)


def token_indicator(count, length):
    width = count * length
    item = lax.broadcasted_iota(jnp.int32, (count, width), 0)
    token = lax.broadcasted_iota(jnp.int32, (count, width), 1)
    start = item * length
    return jnp.where((token >= start) & (token < start + length), 1.0, 0.0).astype(BF16)


def position():
    return lax.axis_index("row") * lax.axis_size("col") + lax.axis_index("col")


def ring_place(row, count):
    if count != 8:
        return row
    side = row % 2
    return (row // 2) * (1 - side) + (7 - row // 2) * side


def ring_row(place, count):
    if count != 8:
        return place
    side = place // 4
    return 2 * (place * (1 - side) + (7 - place) * side) + side


def gather_kernel(
    dims, count, pattern_ref, own_c_ref, own_q_ref, full_c_ref, full_q_ref, full_s_ref,
    mine_ref, lse_ref, hop_send, hop_recv, push_send, push_recv, score_send, score_recv, local_sem, pattern_smem,
):
    block, length, chunk = dims
    tokens = block * length
    own = (own_c_ref, own_q_ref)
    full = (full_c_ref, full_q_ref)
    rows = (tokens, tokens, block)
    clause, query, score = 0, 1, 2
    row, core = lax.axis_index("row"), lax.axis_index("col")
    sibling = {"col": 1 - core}
    place = ring_place(row, count)
    ahead = {"row": ring_row((place + 1) % count, count)}
    behind = {"row": ring_row((place + count - 1) % count, count)}
    last = count // 2

    def source_row(way, step):
        return ring_row((place + count + (2 * way - 1) * step) % count, count)

    def block_start(a, source):
        return pl.multiple_of((source * 2 + core) * rows[a], rows[a])

    def piece(a, way, step):
        if step < last:
            return 0, rows[a]
        return way * (rows[a] // 2), rows[a] // 2

    def hop(a, way, step):
        offset, size = piece(a, way, step)
        start = block_start(a, source_row(way, step - 1)) + offset
        target = full[a].at[pl.ds(start, size), :]
        return pltpu.make_async_remote_copy(
            src_ref=own[a].at[pl.ds(offset, size), :] if step == 1 else target,
            dst_ref=target,
            send_sem=hop_send.at[a, way, step - 1],
            recv_sem=hop_recv.at[a, way, step - 1],
            device_id=ahead if way == 0 else behind,
            device_id_type=pl.DeviceIdType.MESH,
        )

    def push(a, way, step):
        offset, size = piece(a, way, step)
        target = full[a].at[pl.ds(block_start(a, source_row(way, step)) + offset, size), :]
        return pltpu.make_async_remote_copy(
            src_ref=own[a] if step == 0 else target,
            dst_ref=target,
            send_sem=push_send.at[a, way, step],
            recv_sem=push_recv.at[a, way, step],
            device_id=sibling,
            device_id_type=pl.DeviceIdType.MESH,
        )

    def begin(a):
        for way in (0, 1):
            hop(a, way, 1).start()
        push(a, 0, 0).start()

    def advance(a, step):
        for way in (0, 1):
            hop(a, way, step).wait_recv()
            if step < last:
                hop(a, way, step + 1).start()
            push(a, way, step).start()

    def score_block(source, side):
        b = source * 2 + side
        for c in range(block // chunk):
            start = pl.multiple_of(b * tokens + c * chunk * length, chunk * length)
            logits = dot(
                full_c_ref[pl.ds(start, chunk * length), :],
                full_q_ref[pl.ds(block_start(query, row), tokens), :],
                ((1,), (1,)),
            ).reshape(chunk, length, tokens)
            top = jnp.max(logits, axis=1, keepdims=True)
            total = jnp.sum(jnp.exp2((logits - top) * EXP2_SCALE), axis=1)
            lse_ref[pl.ds(pl.multiple_of(b * block + c * chunk, chunk), chunk), :] = (
                top.reshape(chunk, tokens) * SHARPNESS + jnp.log(total)
            )

    def score_arrived(step, side):
        @pl.loop(0, 1 if step == last or step == 0 else 2)
        def _(way):
            score_block(source_row(way, step), side)

    devices = 2 * count
    me = row * 2 + core

    def peer(distance):
        target = (me + distance) % devices
        return {"row": target // 2, "col": target % 2}

    def send_scores(distance):
        return pltpu.make_async_remote_copy(
            src_ref=mine_ref,
            dst_ref=full_s_ref.at[pl.ds(block_start(score, row), block), :],
            send_sem=score_send.at[distance - 1],
            recv_sem=score_recv.at[distance - 1],
            device_id=peer(distance),
            device_id_type=pl.DeviceIdType.MESH,
        )

    barrier = pltpu.get_barrier_semaphore()
    for distance in range(1, devices):
        pl.semaphore_signal(barrier, inc=1, device_id=peer(distance), device_id_type=pl.DeviceIdType.MESH)
    locals_ = [
        pltpu.make_async_copy(own[a], full[a].at[pl.ds(block_start(a, row), tokens), :], local_sem.at[a])
        for a in (clause, query)
    ]
    pattern_copy = pltpu.make_async_copy(pattern_ref, pattern_smem, local_sem.at[2])
    pattern_copy.start()
    for copy in locals_:
        copy.start()
    pl.semaphore_wait(barrier, devices - 1)

    begin(clause)
    begin(query)
    for copy in locals_:
        copy.wait()
    score_arrived(0, core)
    push(clause, 0, 0).wait()
    score_arrived(0, 1 - core)
    for step in range(1, last + 1):
        advance(clause, step)
        score_arrived(step, core)
        if step < last:
            advance(query, step)
        for way in (0, 1):
            push(clause, way, step).wait()
        score_arrived(step, 1 - core)

    pattern_copy.wait()
    blocks = full_c_ref.shape[0] // tokens
    lane = lax.broadcasted_iota(jnp.int32, mine_ref.shape, 1)
    mask = jnp.zeros(mine_ref.shape, jnp.int32)
    for b in range(blocks):
        mask = jnp.where((lane >= b * block) & (lane < (b + 1) * block), pattern_smem[me, b], mask)
    indicator = token_indicator(block, length)
    hi, mid, low = split3(lse_ref[...])
    sums = dot(indicator, hi, ((1,), (1,))) + (
        dot(indicator, mid, ((1,), (1,))) + dot(indicator, low, ((1,), (1,)))
    )
    mine_ref[...] = jnp.where(mask > 0, sums / SHARPNESS, FLOOR_VALUE)
    for distance in range(1, devices):
        send_scores(distance).start()
    full_s_ref[pl.ds(block_start(score, row), block), :] = mine_ref[...]

    advance(query, last)
    for distance in range(1, devices):
        send_scores(distance).wait()
    push(query, 0, 0).wait()
    for step in range(1, last + 1):
        for way in (0, 1):
            hop(clause, way, step).wait_send()
            hop(query, way, step).wait_send()
            push(query, way, step).wait()


def softmax_weights(logits, factor, chunk, length):
    logits = logits.reshape(chunk, length, logits.shape[1])
    top = jnp.max(logits, axis=1, keepdims=True)
    raised = jnp.exp2((logits - top) * EXP2_SCALE)
    total = jnp.sum(raised, axis=1)
    weights = raised * (factor / total)[:, None, :]
    return weights.reshape(chunk * length, logits.shape[2]).astype(BF16)


def grad_kernel(
    dims, pattern_hbm, positive_hbm, queries_ref, clauses_ref, scores_ref,
    per_query_ref, grad_q_ref, grad_c_ref,
    row_factor_ref, col_factor_ref, weights_ref, grad_qt_ref, pattern_ref, positive_ref, local_sem,
):
    pattern_copy = pltpu.make_async_copy(pattern_hbm, pattern_ref, local_sem.at[0])
    positive_copy = pltpu.make_async_copy(positive_hbm, positive_ref, local_sem.at[1])
    pattern_copy.start()
    positive_copy.start()
    block, length, chunk = dims
    place = position()
    tokens = block * length
    blocks = clauses_ref.shape[0] // tokens
    own = pl.multiple_of(place * block, block)
    own_start = pl.multiple_of(place * tokens, tokens)
    indicator = token_indicator(block, length)
    total_rows = scores_ref.shape[0]

    scores = scores_ref[...]
    row_top = jnp.max(scores, axis=1, keepdims=True)
    row_lse = row_top + jnp.log(jnp.sum(jnp.exp(scores - row_top), axis=1, keepdims=True))
    col_top = jnp.max(scores, axis=0, keepdims=True)
    col_lse = col_top + jnp.log(jnp.sum(jnp.exp(scores - col_top), axis=0, keepdims=True))

    mine = scores_ref[pl.ds(own, block), :]
    mine_top = jnp.max(mine, axis=1, keepdims=True)
    mine_lse = mine_top + jnp.log(jnp.sum(jnp.exp(mine - mine_top), axis=1, keepdims=True))
    pattern_copy.wait()
    positive_copy.wait()
    item = lax.broadcasted_iota(jnp.int32, (block, 1), 0)
    positive = jnp.zeros((block, 1), jnp.int32)
    for i in range(block):
        positive = jnp.where(item == i, positive_ref[i], positive)
    matches = positive == lax.broadcasted_iota(jnp.int32, (block, total_rows), 1)
    positive_score = jnp.sum(jnp.where(matches, mine, 0.0), axis=1, keepdims=True)
    positive_col = jnp.sum(jnp.where(matches, col_lse, 0.0), axis=1, keepdims=True)
    per_query = 0.5 * (mine_lse - positive_score) + 0.5 * (positive_col - positive_score)
    per_query_ref[...] = jnp.sum(
        jnp.where(item == lax.broadcasted_iota(jnp.int32, (block, block), 1), per_query, 0.0),
        axis=0,
        keepdims=True,
    )

    row_factor = 0.5 * (jnp.exp(mine - mine_lse) + jnp.exp(mine - col_lse)) - jnp.where(matches, 1.0, 0.0)
    row_factor_ref[...] = exact_dot(split3(row_factor), indicator, ((0,), (0,)))

    factor = 0.5 * (jnp.exp(scores - row_lse) + jnp.exp(scores - col_lse))
    col_factor_ref[...] = pltpu.roll(factor, total_rows - own, 1)[:, :128]
    local = positive - own == lax.broadcasted_iota(jnp.int32, (block, 128), 1)
    col_factor_ref[pl.ds(own, block), :] = col_factor_ref[pl.ds(own, block), :] - jnp.where(local, 1.0, 0.0)

    grad_qt_ref[...] = jnp.zeros_like(grad_qt_ref)
    grad_c_ref[...] = jnp.zeros_like(grad_c_ref)

    @pl.loop(0, blocks)
    def _(b):
        base = pl.multiple_of(b * tokens, tokens)

        @pl.when(pattern_ref[place, b] > 0)
        def _():
            for c in range(block // chunk):
                start = pl.multiple_of(base + c * chunk * length, chunk * length)
                logits = dot(clauses_ref[pl.ds(start, chunk * length), :], queries_ref[pl.ds(own_start, tokens), :], ((1,), (1,)))
                factor_tile = row_factor_ref[pl.ds(pl.multiple_of(b * block + c * chunk, chunk), chunk), :]
                weights_ref[pl.ds(c * chunk * length, chunk * length), :] = softmax_weights(
                    logits, factor_tile, chunk, length
                )
            grad_qt_ref[...] += dot(clauses_ref[pl.ds(base, tokens), :], weights_ref[...], ((0,), (0,)))

        @pl.when(pattern_ref[b, place] > 0)
        def _():
            block_factor = col_factor_ref[pl.ds(pl.multiple_of(b * block, block), block), :][:, :block]
            spread = exact_dot(split3(block_factor), indicator, ((0,), (0,)))
            query_tile = queries_ref[pl.ds(base, tokens), :]
            for c in range(block // chunk):
                logits = dot(clauses_ref[pl.ds(pl.multiple_of(own_start + c * chunk * length, chunk * length), chunk * length), :], query_tile, ((1,), (1,)))
                weights_ref[pl.ds(c * chunk * length, chunk * length), :] = softmax_weights(
                    logits, spread[c * chunk : (c + 1) * chunk], chunk, length
                )
            grad_c_ref[...] += dot(weights_ref[...], query_tile, ((1,), (0,)))

    grad_q_ref[...] = grad_qt_ref[...].T


def shards(queries, clauses, pattern, positive):
    block, length, width = queries.shape
    blocks = pattern.shape[0]
    tokens = block * length
    total_rows = blocks * block
    dims = (block, length, 8)
    own_q = queries.reshape(tokens, width)
    own_c = clauses.reshape(tokens, width)
    count = lax.axis_size("row")
    vmem = pl.BlockSpec(memory_space=pltpu.VMEM)
    anywhere = pl.BlockSpec(memory_space=pltpu.HBM)
    sems = pltpu.SemaphoreType.DMA
    all_c, all_q, all_scores = pl.pallas_call(
        functools.partial(gather_kernel, dims, count),
        out_shape=(
            jax.ShapeDtypeStruct((blocks * tokens, width), BF16),
            jax.ShapeDtypeStruct((blocks * tokens, width), BF16),
            jax.ShapeDtypeStruct((total_rows, total_rows), F32),
        ),
        in_specs=[anywhere] * 3,
        out_specs=(vmem, vmem, vmem),
        scratch_shapes=[
            pltpu.VMEM((block, total_rows), F32),
            pltpu.VMEM((total_rows, tokens), F32),
            sems((2, 2, count // 2)),
            sems((2, 2, count // 2)),
            sems((2, 2, count // 2 + 1)),
            sems((2, 2, count // 2 + 1)),
            sems((blocks - 1,)),
            sems((blocks - 1,)),
            sems((3,)),
            pltpu.SMEM(pattern.shape, jnp.int32),
        ],
        compiler_params=pltpu.CompilerParams(
            collective_id=0, has_side_effects=True, vmem_limit_bytes=40 * 1024 * 1024
        ),
        name="gather_scores",
    )(pattern, own_c, own_q)
    per_query, grad_q, grad_c = pl.pallas_call(
        functools.partial(grad_kernel, (block, length, block)),
        out_shape=(
            jax.ShapeDtypeStruct((1, block), F32),
            jax.ShapeDtypeStruct((tokens, width), F32),
            jax.ShapeDtypeStruct((tokens, width), F32),
        ),
        in_specs=[anywhere, anywhere, vmem, vmem, vmem],
        out_specs=(vmem, vmem, vmem),
        scratch_shapes=[
            pltpu.VMEM((total_rows, tokens), F32),
            pltpu.VMEM((total_rows, 128), F32),
            pltpu.VMEM((tokens, tokens), BF16),
            pltpu.VMEM((width, tokens), F32),
            pltpu.SMEM(pattern.shape, jnp.int32),
            pltpu.SMEM(positive.shape, jnp.int32),
            sems((2,)),
        ],
        compiler_params=pltpu.CompilerParams(vmem_limit_bytes=40 * 1024 * 1024),
        name="grads",
    )(pattern, positive, all_q, all_c, all_scores)
    return (
        per_query.reshape(block),
        grad_q.reshape(queries.shape),
        grad_c.reshape(clauses.shape),
    )


def solution(mesh):
    rows = P(("groups", "row", "col"), None, None)
    ids = P(("groups", "row", "col"))
    return jax.shard_map(
        shards,
        mesh=mesh,
        in_specs=(rows, rows, P("groups", None), ids),
        out_specs=(ids, rows, rows),
        check_vma=False,
    )
```

```python
import functools
import math

import jax
import jax.numpy as jnp
from jax import lax
from jax.experimental import pallas as pl
from jax.experimental.pallas import tpu as pltpu
from jax.sharding import PartitionSpec as P

SHARPNESS = 3.0
FLOOR_VALUE = -1e30
EXP2_SCALE = SHARPNESS * math.log2(math.e)
LN2 = math.log(2.0)
F32 = jnp.float32
BF16 = jnp.bfloat16


def dot(a, b, dims):
    return lax.dot_general(a, b, (dims, ((), ())), preferred_element_type=F32)


def split3(x):
    hi = x.astype(BF16)
    rest = x - hi.astype(F32)
    mid = rest.astype(BF16)
    return hi, mid, (rest - mid.astype(F32)).astype(BF16)


def exact_dot(parts, other, dims):
    hi, mid, low = (dot(part, other, dims) for part in parts)
    return hi + (mid + low)


def token_indicator(count, length):
    width = count * length
    item = lax.broadcasted_iota(jnp.int32, (count, width), 0)
    token = lax.broadcasted_iota(jnp.int32, (count, width), 1)
    start = item * length
    return jnp.where((token >= start) & (token < start + length), 1.0, 0.0).astype(BF16)


def position():
    return lax.axis_index("row") * lax.axis_size("col") + lax.axis_index("col")


def ring_place(row, count):
    if count != 8:
        return row
    side = row % 2
    return (row // 2) * (1 - side) + (7 - row // 2) * side


def ring_row(place, count):
    if count != 8:
        return place
    side = place // 4
    return 2 * (place * (1 - side) + (7 - place) * side) + side


def gather_kernel(
    dims, count, pattern_ref, own_c_ref, own_q_ref, full_c_ref, full_q_ref, full_s_ref,
    mine_ref, lse_ref, hop_send, hop_recv, push_send, push_recv, score_send, score_recv, local_sem, pattern_smem,
):
    block, length, chunk = dims
    tokens = block * length
    own = (own_c_ref, own_q_ref)
    full = (full_c_ref, full_q_ref)
    rows = (tokens, tokens, block)
    clause, query, score = 0, 1, 2
    row, core = lax.axis_index("row"), lax.axis_index("col")
    sibling = {"col": 1 - core}
    place = ring_place(row, count)
    ahead = {"row": ring_row((place + 1) % count, count)}
    behind = {"row": ring_row((place + count - 1) % count, count)}
    last = count // 2

    def source_row(way, step):
        return ring_row((place + count + (2 * way - 1) * step) % count, count)

    def block_start(a, source):
        return pl.multiple_of((source * 2 + core) * rows[a], rows[a])

    def piece(a, way, step):
        if step < last:
            return 0, rows[a]
        return way * (rows[a] // 2), rows[a] // 2

    def hop(a, way, step):
        offset, size = piece(a, way, step)
        start = block_start(a, source_row(way, step - 1)) + offset
        target = full[a].at[pl.ds(start, size), :]
        return pltpu.make_async_remote_copy(
            src_ref=own[a].at[pl.ds(offset, size), :] if step == 1 else target,
            dst_ref=target,
            send_sem=hop_send.at[a, way, step - 1],
            recv_sem=hop_recv.at[a, way, step - 1],
            device_id=ahead if way == 0 else behind,
            device_id_type=pl.DeviceIdType.MESH,
        )

    def push(a, way, step):
        offset, size = piece(a, way, step)
        target = full[a].at[pl.ds(block_start(a, source_row(way, step)) + offset, size), :]
        return pltpu.make_async_remote_copy(
            src_ref=own[a] if step == 0 else target,
            dst_ref=target,
            send_sem=push_send.at[a, way, step],
            recv_sem=push_recv.at[a, way, step],
            device_id=sibling,
            device_id_type=pl.DeviceIdType.MESH,
        )

    def begin(a):
        for way in (0, 1):
            hop(a, way, 1).start()
        push(a, 0, 0).start()

    def advance(a, step):
        for way in (0, 1):
            hop(a, way, step).wait_recv()
            if step < last:
                hop(a, way, step + 1).start()
            push(a, way, step).start()

    def score_block(source, side):
        b = source * 2 + side
        for c in range(block // chunk):
            start = pl.multiple_of(b * tokens + c * chunk * length, chunk * length)
            logits = dot(
                full_c_ref[pl.ds(start, chunk * length), :],
                full_q_ref[pl.ds(block_start(query, row), tokens), :],
                ((1,), (1,)),
            ).reshape(chunk, length, tokens)
            top = jnp.max(logits, axis=1, keepdims=True)
            total = jnp.sum(jnp.exp2((logits - top) * EXP2_SCALE), axis=1)
            lse_ref[pl.ds(pl.multiple_of(b * block + c * chunk, chunk), chunk), :] = (
                top.reshape(chunk, tokens) * SHARPNESS + jnp.log(total)
            )

    def score_arrived(step, side):
        @pl.loop(0, 1 if step == last or step == 0 else 2)
        def _(way):
            score_block(source_row(way, step), side)

    devices = 2 * count
    me = row * 2 + core

    def peer(distance):
        target = (me + distance) % devices
        return {"row": target // 2, "col": target % 2}

    def send_scores(distance):
        return pltpu.make_async_remote_copy(
            src_ref=mine_ref,
            dst_ref=full_s_ref.at[pl.ds(block_start(score, row), block), :],
            send_sem=score_send.at[distance - 1],
            recv_sem=score_recv.at[distance - 1],
            device_id=peer(distance),
            device_id_type=pl.DeviceIdType.MESH,
        )

    barrier = pltpu.get_barrier_semaphore()
    for distance in range(1, devices):
        pl.semaphore_signal(barrier, inc=1, device_id=peer(distance), device_id_type=pl.DeviceIdType.MESH)
    locals_ = [
        pltpu.make_async_copy(own[a], full[a].at[pl.ds(block_start(a, row), tokens), :], local_sem.at[a])
        for a in (clause, query)
    ]
    pattern_copy = pltpu.make_async_copy(pattern_ref, pattern_smem, local_sem.at[2])
    pattern_copy.start()
    for copy in locals_:
        copy.start()
    pl.semaphore_wait(barrier, devices - 1)

    begin(clause)
    begin(query)
    for copy in locals_:
        copy.wait()
    score_arrived(0, core)
    push(clause, 0, 0).wait()
    score_arrived(0, 1 - core)
    for step in range(1, last + 1):
        advance(clause, step)
        score_arrived(step, core)
        if step < last:
            advance(query, step)
        for way in (0, 1):
            push(clause, way, step).wait()
        score_arrived(step, 1 - core)

    pattern_copy.wait()
    blocks = full_c_ref.shape[0] // tokens
    lane = lax.broadcasted_iota(jnp.int32, mine_ref.shape, 1)
    mask = jnp.zeros(mine_ref.shape, jnp.int32)
    for b in range(blocks):
        mask = jnp.where((lane >= b * block) & (lane < (b + 1) * block), pattern_smem[me, b], mask)
    indicator = token_indicator(block, length)
    hi, mid, low = split3(lse_ref[...])
    sums = dot(indicator, hi, ((1,), (1,))) + (
        dot(indicator, mid, ((1,), (1,))) + dot(indicator, low, ((1,), (1,)))
    )
    mine_ref[...] = jnp.where(mask > 0, sums / SHARPNESS, FLOOR_VALUE)
    for distance in range(1, devices):
        send_scores(distance).start()
    full_s_ref[pl.ds(block_start(score, row), block), :] = mine_ref[...]

    advance(query, last)
    for distance in range(1, devices):
        send_scores(distance).wait()
    push(query, 0, 0).wait()
    for step in range(1, last + 1):
        for way in (0, 1):
            hop(clause, way, step).wait_send()
            hop(query, way, step).wait_send()
            push(query, way, step).wait()


def softmax_weights(logits, factor, chunk, length):
    logits = logits.reshape(chunk, length, logits.shape[1])
    top = jnp.max(logits, axis=1, keepdims=True)
    raised = jnp.exp2((logits - top) * EXP2_SCALE)
    total = jnp.sum(raised, axis=1)
    weights = raised * (factor / total)[:, None, :]
    return weights.reshape(chunk * length, logits.shape[2]).astype(BF16)


def grad_kernel(
    dims, pattern_hbm, positive_hbm, queries_ref, clauses_ref, scores_ref,
    per_query_ref, grad_q_ref, grad_c_ref,
    row_factor_ref, col_factor_ref, weights_ref, grad_qt_ref, pattern_ref, positive_ref, local_sem,
):
    pattern_copy = pltpu.make_async_copy(pattern_hbm, pattern_ref, local_sem.at[0])
    positive_copy = pltpu.make_async_copy(positive_hbm, positive_ref, local_sem.at[1])
    pattern_copy.start()
    positive_copy.start()
    block, length, chunk = dims
    place = position()
    tokens = block * length
    blocks = clauses_ref.shape[0] // tokens
    own = pl.multiple_of(place * block, block)
    own_start = pl.multiple_of(place * tokens, tokens)
    indicator = token_indicator(block, length)
    total_rows = scores_ref.shape[0]

    scores = scores_ref[...]
    row_top = jnp.max(scores, axis=1, keepdims=True)
    row_lse = row_top + jnp.log(jnp.sum(jnp.exp(scores - row_top), axis=1, keepdims=True))
    col_top = jnp.max(scores, axis=0, keepdims=True)
    col_lse = col_top + jnp.log(jnp.sum(jnp.exp(scores - col_top), axis=0, keepdims=True))

    mine = scores_ref[pl.ds(own, block), :]
    mine_top = jnp.max(mine, axis=1, keepdims=True)
    mine_lse = mine_top + jnp.log(jnp.sum(jnp.exp(mine - mine_top), axis=1, keepdims=True))
    pattern_copy.wait()
    positive_copy.wait()
    item = lax.broadcasted_iota(jnp.int32, (block, 1), 0)
    positive = jnp.zeros((block, 1), jnp.int32)
    for i in range(block):
        positive = jnp.where(item == i, positive_ref[i], positive)
    matches = positive == lax.broadcasted_iota(jnp.int32, (block, total_rows), 1)
    positive_score = jnp.sum(jnp.where(matches, mine, 0.0), axis=1, keepdims=True)
    positive_col = jnp.sum(jnp.where(matches, col_lse, 0.0), axis=1, keepdims=True)
    per_query = 0.5 * (mine_lse - positive_score) + 0.5 * (positive_col - positive_score)
    per_query_ref[...] = jnp.sum(
        jnp.where(item == lax.broadcasted_iota(jnp.int32, (block, block), 1), per_query, 0.0),
        axis=0,
        keepdims=True,
    )

    row_factor = 0.5 * (jnp.exp(mine - mine_lse) + jnp.exp(mine - col_lse)) - jnp.where(matches, 1.0, 0.0)
    row_factor_ref[...] = exact_dot(split3(row_factor), indicator, ((0,), (0,)))

    factor = 0.5 * (jnp.exp(scores - row_lse) + jnp.exp(scores - col_lse))
    col_factor_ref[...] = pltpu.roll(factor, total_rows - own, 1)[:, :128]
    local = positive - own == lax.broadcasted_iota(jnp.int32, (block, 128), 1)
    col_factor_ref[pl.ds(own, block), :] = col_factor_ref[pl.ds(own, block), :] - jnp.where(local, 1.0, 0.0)

    grad_qt_ref[...] = jnp.zeros_like(grad_qt_ref)
    grad_c_ref[...] = jnp.zeros_like(grad_c_ref)

    @pl.loop(0, blocks)
    def _(b):
        base = pl.multiple_of(b * tokens, tokens)

        @pl.when(pattern_ref[place, b] > 0)
        def _():
            for c in range(block // chunk):
                start = pl.multiple_of(base + c * chunk * length, chunk * length)
                logits = dot(clauses_ref[pl.ds(start, chunk * length), :], queries_ref[pl.ds(own_start, tokens), :], ((1,), (1,)))
                factor_tile = row_factor_ref[pl.ds(pl.multiple_of(b * block + c * chunk, chunk), chunk), :]
                weights_ref[pl.ds(c * chunk * length, chunk * length), :] = softmax_weights(
                    logits, factor_tile, chunk, length
                )
            grad_qt_ref[...] += dot(clauses_ref[pl.ds(base, tokens), :], weights_ref[...], ((0,), (0,)))

        @pl.when(pattern_ref[b, place] > 0)
        def _():
            block_factor = col_factor_ref[pl.ds(pl.multiple_of(b * block, block), block), :][:, :block]
            spread = exact_dot(split3(block_factor), indicator, ((0,), (0,)))
            query_tile = queries_ref[pl.ds(base, tokens), :]
            for c in range(block // chunk):
                logits = dot(clauses_ref[pl.ds(pl.multiple_of(own_start + c * chunk * length, chunk * length), chunk * length), :], query_tile, ((1,), (1,)))
                weights_ref[pl.ds(c * chunk * length, chunk * length), :] = softmax_weights(
                    logits, spread[c * chunk : (c + 1) * chunk], chunk, length
                )
            grad_c_ref[...] += dot(weights_ref[...], query_tile, ((1,), (0,)))

    grad_q_ref[...] = grad_qt_ref[...].T


def shards(queries, clauses, pattern, positive):
    block, length, width = queries.shape
    blocks = pattern.shape[0]
    tokens = block * length
    total_rows = blocks * block
    dims = (block, length, block)
    own_q = queries.reshape(tokens, width)
    own_c = clauses.reshape(tokens, width)
    count = lax.axis_size("row")
    vmem = pl.BlockSpec(memory_space=pltpu.VMEM)
    anywhere = pl.BlockSpec(memory_space=pltpu.HBM)
    sems = pltpu.SemaphoreType.DMA
    all_c, all_q, all_scores = pl.pallas_call(
        functools.partial(gather_kernel, dims, count),
        out_shape=(
            jax.ShapeDtypeStruct((blocks * tokens, width), BF16),
            jax.ShapeDtypeStruct((blocks * tokens, width), BF16),
            jax.ShapeDtypeStruct((total_rows, total_rows), F32),
        ),
        in_specs=[anywhere] * 3,
        out_specs=(vmem, vmem, vmem),
        scratch_shapes=[
            pltpu.VMEM((block, total_rows), F32),
            pltpu.VMEM((total_rows, tokens), F32),
            sems((2, 2, count // 2)),
            sems((2, 2, count // 2)),
            sems((2, 2, count // 2 + 1)),
            sems((2, 2, count // 2 + 1)),
            sems((blocks - 1,)),
            sems((blocks - 1,)),
            sems((3,)),
            pltpu.SMEM(pattern.shape, jnp.int32),
        ],
        compiler_params=pltpu.CompilerParams(
            collective_id=0, has_side_effects=True, vmem_limit_bytes=40 * 1024 * 1024
        ),
        name="gather_scores",
    )(pattern, own_c, own_q)
    per_query, grad_q, grad_c = pl.pallas_call(
        functools.partial(grad_kernel, dims),
        out_shape=(
            jax.ShapeDtypeStruct((1, block), F32),
            jax.ShapeDtypeStruct((tokens, width), F32),
            jax.ShapeDtypeStruct((tokens, width), F32),
        ),
        in_specs=[anywhere, anywhere, vmem, vmem, vmem],
        out_specs=(vmem, vmem, vmem),
        scratch_shapes=[
            pltpu.VMEM((total_rows, tokens), F32),
            pltpu.VMEM((total_rows, 128), F32),
            pltpu.VMEM((tokens, tokens), BF16),
            pltpu.VMEM((width, tokens), F32),
            pltpu.SMEM(pattern.shape, jnp.int32),
            pltpu.SMEM(positive.shape, jnp.int32),
            sems((2,)),
        ],
        compiler_params=pltpu.CompilerParams(vmem_limit_bytes=40 * 1024 * 1024),
        name="grads",
    )(pattern, positive, all_q, all_c, all_scores)
    return (
        per_query.reshape(block),
        grad_q.reshape(queries.shape),
        grad_c.reshape(clauses.shape),
    )


def solution(mesh):
    rows = P(("groups", "row", "col"), None, None)
    ids = P(("groups", "row", "col"))
    return jax.shard_map(
        shards,
        mesh=mesh,
        in_specs=(rows, rows, P("groups", None), ids),
        out_specs=(ids, rows, rows),
        check_vma=False,
    )
```
